256 devices in a mesh: src: 16 (over x, y_lo, core), rcv: 16 (over z, y_hi).
Axes of the slice: x: 4, y: 4 (y_hi: 2, y_lo: 2; y = y_hi * 2 + y_lo), z: 8, core: 2. Of those that a mesh axis runs over, the one named last changes fastest.
Arguments:
- data: bfloat16 [2, 6144, 6144], P(None, 'src', 'rcv'), may hold values from -24 to 24
- source_term: float32 [2, 6144], P(None, 'src'), may hold values from -1 to 1
Outputs:
- matched: bfloat16 [2, 6144, 6144], P(None, 'src', 'rcv')
The draws below stay inside these ranges and needn't reach their ends.
All inputs are finite; a program needn't handle non-finite values.
Results may differ from the reference program's by a relative error of at most 0.0057.
Values may be sent and summed in bfloat16 or wider, within the bound.
No kernel may reach another device: no remote copies, remote signals or barrier semaphores. Data moves between devices by JAX's collectives and lax.ppermute only.
A program may use at most 64 MiB of HBM per device.

```python
import math
import jax
import jax.numpy as jnp

NS = 6144
LINE = 64


def source_values(key):
    base = jax.random.fold_in(key, 101)
    key_amp, key_phase = jax.random.split(base)
    amplitude = jnp.exp(jax.random.uniform(key_amp, (NS,), jnp.float32, math.log(0.5), math.log(2.0))) / math.sqrt(NS)
    phase = jax.random.uniform(key_phase, (NS,), jnp.float32, -math.pi, math.pi)
    return jnp.stack([amplitude * jnp.cos(phase), amplitude * jnp.sin(phase)])


def draw_source_term(key, part):
    return source_values(key)


def draw_data(key, part):
    weights = source_values(key)
    base = jax.random.fold_in(key, 202)
    key_wave, key_gain = jax.random.split(base)
    direct = 0.5 * jax.random.normal(key_wave, (2, NS, NS), jnp.float32)
    gain_low = 0.25
    right_re = weights[0][:, None] * direct[0] - weights[1][:, None] * direct[1]
    right_im = weights[0][:, None] * direct[1] + weights[1][:, None] * direct[0]
    echo_re = jnp.dot(direct[0], right_re) - jnp.dot(direct[1], right_im)
    echo_im = jnp.dot(direct[0], right_im) + jnp.dot(direct[1], right_re)
    lines = NS // LINE
    gain = jnp.exp(jax.random.uniform(key_gain, (lines, lines), jnp.float32, math.log(gain_low), math.log(2.5)))
    spread = jnp.repeat(jnp.repeat(gain, LINE, axis=0), LINE, axis=1)
    return (spread[None] * (direct + jnp.stack([echo_re, echo_im]))).astype(jnp.bfloat16)


def setup_inputs(seed: int = 0) -> dict:
    splits = jax.random.split(jax.random.key(seed), 3)
    data = draw_data(jax.random.fold_in(splits[2], 71), 0)
    source_term = draw_source_term(jax.random.fold_in(splits[2], 71), 0)
    return {"data": data, "source_term": source_term}


def line_block_sums(multiples, data):
    mult = multiples.astype(jnp.float32)
    recorded = data.astype(jnp.float32)
    cross_re = mult[0] * recorded[0] + mult[1] * recorded[1]
    cross_im = mult[0] * recorded[1] - mult[1] * recorded[0]
    energy = mult[0] * mult[0] + mult[1] * mult[1]
    stacked = jnp.stack([cross_re, cross_im, energy])
    height = stacked.shape[1] // LINE
    breadth = stacked.shape[2] // LINE
    return stacked.reshape(3, height, LINE, breadth, LINE).sum(axis=(2, 4))


def reference(data, source_term):
    recorded = data.astype(jnp.float32)
    weight_re = source_term[0][:, None]
    weight_im = source_term[1][:, None]
    scaled_re = (weight_re * recorded[0] - weight_im * recorded[1]).astype(jnp.bfloat16)
    scaled_im = (weight_re * recorded[1] + weight_im * recorded[0]).astype(jnp.bfloat16)
    product_re = jnp.dot(data[0], scaled_re, preferred_element_type=jnp.float32) - jnp.dot(data[1], scaled_im, preferred_element_type=jnp.float32)
    product_im = jnp.dot(data[0], scaled_im, preferred_element_type=jnp.float32) + jnp.dot(data[1], scaled_re, preferred_element_type=jnp.float32)
    multiples = jnp.stack([product_re, product_im]).astype(jnp.bfloat16)
    sums = line_block_sums(multiples, data)
    count = sums.shape[1]
    padded = jnp.pad(sums, ((0, 0), (1, 1), (1, 1)))
    window = jnp.zeros_like(sums)
    for shift_row in range(3):
        for shift_col in range(3):
            window = window + padded[:, shift_row:shift_row + count, shift_col:shift_col + count]
    filter_re = window[0] / (window[2] + 1e-5)
    filter_im = window[1] / (window[2] + 1e-5)
    mult = multiples.astype(jnp.float32).reshape(2, count, LINE, count, LINE)
    coef_re = filter_re[:, None, :, None]
    coef_im = filter_im[:, None, :, None]
    matched_re = coef_re * mult[0] - coef_im * mult[1]
    matched_im = coef_re * mult[1] + coef_im * mult[0]
    matched = jnp.stack([matched_re, matched_im]).reshape(2, NS, NS)
    return matched.astype(jnp.bfloat16)
```

```python
import jax
import jax.numpy as jnp
from jax import lax
from jax.experimental import pallas as pl
from jax.experimental.pallas import tpu as pltpu
from jax.sharding import PartitionSpec as P

LINE = 64
STABILISER = 1e-05
AXES = ("src", "rcv")
NX, NY, NZ = 4, 4, 8
CHUNKS = 2


def linear(x, y, z, core):
    return ((x * 2 + y % 2) * 2 + core) * 16 + z * 2 + y // 2


def send(value, target):
    pairs = []
    for x in range(NX):
        for y in range(NY):
            for z in range(NZ):
                for core in range(2):
                    to = target(x, y, z, core)
                    if to is not None:
                        pairs.append((linear(x, y, z, core), linear(to[0] % NX, to[1] % NY, to[2] % NZ, to[3])))
    return lax.ppermute(value, AXES, pairs)


def x_up(x, y, z, core):
    return x + 1, y, z, core


def x_down(x, y, z, core):
    return x - 1, y, z, core


def z_up(x, y, z, core):
    return x, y, z + 1, core


def z_down(x, y, z, core):
    return x, y, z - 1, core


def y_across(x, y, z, core):
    return x, y + 2, z, core


def swap_core(x, y, z, core):
    return x, y, z, 1 - core


def near_y(x, y, z, core):
    if y // 2 == core:
        return x, y ^ 1, z, 1 - core
    return x, 3 - y, z, core


def far_y(x, y, z, core):
    if y // 2 == core:
        return None
    return x, y ^ 2, z, 1 - core


def scale_kernel(data_ref, source_ref, out_ref):
    weights = jnp.transpose(jnp.concatenate([source_ref[...]] * 4, axis=0))
    weight_re = weights[:, 0:1]
    weight_im = weights[:, 1:2]
    recorded_re = data_ref[0].astype(jnp.float32)
    recorded_im = data_ref[1].astype(jnp.float32)
    width = recorded_re.shape[1]
    out_ref[:, :width] = (weight_re * recorded_re - weight_im * recorded_im).astype(jnp.bfloat16)
    out_ref[:, width:] = (weight_re * recorded_im + weight_im * recorded_re).astype(jnp.bfloat16)


def scale(data, source_term):
    _, rows, cols = data.shape
    return pl.pallas_call(
        scale_kernel,
        out_shape=jax.ShapeDtypeStruct((rows, 2 * cols), jnp.bfloat16),
        in_specs=[pl.BlockSpec(memory_space=pltpu.VMEM)] * 2,
        out_specs=pl.BlockSpec(memory_space=pltpu.VMEM),
        cost_estimate=pl.CostEstimate(flops=6 * rows * cols, bytes_accessed=8 * rows * cols, transcendentals=0),
        name="scale",
    )(data, source_term)


def product_kernel(place_ref, *refs):
    left = refs[:8]
    right = refs[8:16]
    out_ref, held, total, sems = refs[16:]
    copies = [pltpu.make_async_copy(left[e], held.at[place_ref[e]], sems.at[e]) for e in range(8)]
    for copy in copies:
        copy.start()
    for copy in copies:
        copy.wait()
    rows, depth = held.shape[2], held.shape[3]
    for s in range(8):
        part = jnp.dot(
            held[s].reshape(2 * rows, depth), right[s][...], preferred_element_type=jnp.float32
        )
        if s == 0:
            total[...] = part
        else:
            total[...] += part
    cols = out_ref.shape[2]
    out_ref[0] = total[:rows, :cols] - total[rows:, cols:]
    out_ref[1] = total[:rows, cols:] + total[rows:, :cols]


def product(place, left, right):
    _, rows, depth = left[0].shape
    cols = right[0].shape[1] // 2
    return pl.pallas_call(
        product_kernel,
        out_shape=jax.ShapeDtypeStruct((2, rows, cols), jnp.float32),
        in_specs=[pl.BlockSpec(memory_space=pltpu.SMEM)]
        + [pl.BlockSpec(memory_space=pl.ANY)] * 8
        + [pl.BlockSpec(memory_space=pltpu.VMEM)] * 8,
        out_specs=pl.BlockSpec(memory_space=pltpu.VMEM),
        scratch_shapes=[
            pltpu.VMEM((8, 2, rows, depth), jnp.bfloat16),
            pltpu.VMEM((2 * rows, 2 * cols), jnp.float32),
            pltpu.SemaphoreType.DMA((8,)),
        ],
        compiler_params=pltpu.CompilerParams(vmem_limit_bytes=24 << 20),
        cost_estimate=pl.CostEstimate(
            flops=8 * 8 * rows * depth * cols, bytes_accessed=8 * 4 * (rows + cols) * depth, transcendentals=0
        ),
        name="product",
    )(place, *left, *right)


def combine_kernel(own_ref, other_ref, data_ref, mult_ref, sums_ref):
    mult_re = (own_ref[0] + other_ref[0]).astype(jnp.bfloat16)
    mult_im = (own_ref[1] + other_ref[1]).astype(jnp.bfloat16)
    mult_ref[0] = mult_re
    mult_ref[1] = mult_im
    rows, cols = mult_re.shape
    lines = rows // LINE
    lane = lax.broadcasted_iota(jnp.int32, (1, cols), 1) // LINE
    slot = lax.broadcasted_iota(jnp.int32, (1, 128), 1)
    for i in range(lines):
        span = slice(i * LINE, (i + 1) * LINE)
        m_re = mult_re[span].astype(jnp.float32)
        m_im = mult_im[span].astype(jnp.float32)
        d_re = data_ref[0, span].astype(jnp.float32)
        d_im = data_ref[1, span].astype(jnp.float32)
        terms = (m_re * d_re + m_im * d_im, m_re * d_im - m_im * d_re, m_re * m_re + m_im * m_im)
        for q, term in enumerate(terms):
            along = jnp.sum(term, axis=0, keepdims=True)
            row = jnp.zeros((1, 128), jnp.float32)
            for j in range(cols // LINE):
                block = jnp.sum(jnp.where(lane == j, along, 0.0), axis=1, keepdims=True)
                row = jnp.where(slot == j, block, row)
            sums_ref[pl.ds(4 * i + q, 1), :] = row
        sums_ref[pl.ds(4 * i + 3, 1), :] = jnp.zeros((1, 128), jnp.float32)


def combine(own, other, data):
    _, rows, cols = own.shape
    return pl.pallas_call(
        combine_kernel,
        out_shape=(
            jax.ShapeDtypeStruct((2, rows, cols), jnp.bfloat16),
            jax.ShapeDtypeStruct((4 * (rows // LINE), 128), jnp.float32),
        ),
        in_specs=[pl.BlockSpec(memory_space=pltpu.VMEM)] * 3,
        out_specs=(pl.BlockSpec(memory_space=pltpu.VMEM),) * 2,
        cost_estimate=pl.CostEstimate(flops=16 * rows * cols, bytes_accessed=24 * rows * cols, transcendentals=0),
        name="combine",
    )(own, other, data)


def apply_kernel(*refs):
    mults = refs[:CHUNKS]
    window_ref, left_ref, right_ref, out_ref = refs[CHUNKS:]
    window = window_ref[...]
    slot = lax.broadcasted_iota(jnp.int32, window.shape, 1)
    last = out_ref.shape[2] // LINE - 1
    before = jnp.where(slot == 0, pltpu.roll(left_ref[...], 128 - last, 1), pltpu.roll(window, 1, 1))
    after = jnp.where(slot == last, pltpu.roll(right_ref[...], last, 1), pltpu.roll(window, 127, 1))
    window = window + before + after
    cols = out_ref.shape[2]
    rows = mults[0].shape[1]
    lane = lax.broadcasted_iota(jnp.int32, (1, cols), 1) // LINE
    for i in range(CHUNKS * rows // LINE):
        energy = window[4 * i + 2 : 4 * i + 3] + STABILISER
        filters = []
        for q in range(2):
            value = window[4 * i + q : 4 * i + q + 1] / energy
            spread = jnp.zeros((1, cols), jnp.float32)
            for j in range(last + 1):
                spread = jnp.where(lane == j, value[:, j : j + 1], spread)
            filters.append(spread)
        coef_re, coef_im = filters
        mult_ref = mults[i * LINE // rows]
        span = pl.ds(i * LINE % rows, LINE)
        m_re = mult_ref[0, span].astype(jnp.float32)
        m_im = mult_ref[1, span].astype(jnp.float32)
        out_ref[0, pl.ds(i * LINE, LINE)] = (coef_re * m_re - coef_im * m_im).astype(jnp.bfloat16)
        out_ref[1, pl.ds(i * LINE, LINE)] = (coef_re * m_im + coef_im * m_re).astype(jnp.bfloat16)


def apply(mults, window, left, right):
    _, rows, cols = mults[0].shape
    return pl.pallas_call(
        apply_kernel,
        out_shape=jax.ShapeDtypeStruct((2, rows * CHUNKS, cols), jnp.bfloat16),
        in_specs=[pl.BlockSpec(memory_space=pltpu.VMEM)] * (CHUNKS + 3),
        out_specs=pl.BlockSpec(memory_space=pltpu.VMEM),
        cost_estimate=pl.CostEstimate(flops=12 * rows * cols, bytes_accessed=16 * rows * cols, transcendentals=0),
        name="apply",
    )(*mults, window, left, right)


def z_gather(pieces):
    slots = [{0: piece} for piece in pieces]
    up = list(pieces)
    down = list(pieces)
    for step in range(1, 5):
        for r in range(len(pieces)):
            if step < 4 or r % 2 == 0:
                up[r] = send(up[r], z_up)
                slots[r][step] = up[r]
            if step < 4 or r % 2 == 1:
                down[r] = send(down[r], z_down)
                slots[r][8 - step] = down[r]
    return [[slot[e] for e in range(8)] for slot in slots]


def x_gather(value):
    half = value.shape[0] // 2
    one = send(value, x_up)
    three = send(value, x_down)
    two = jnp.concatenate([send(one[:half], x_up), send(three[half:], x_down)], axis=0)
    ring = [value, one, two, three]
    return ring + [send(part, swap_core) for part in ring]


def on_device(data, source_term):
    rows = data.shape[1]
    src = lax.axis_index("src")
    rcv = lax.axis_index("rcv")
    x, y_lo, core = src // 4, (src // 2) % 2, src % 2
    z, y_hi = rcv // 2, rcv % 2
    home = core == y_hi
    block = (z - jnp.arange(8, dtype=jnp.int32)) % 8
    shift_x = (x - block // 2) % 4
    shift_y = (block % 2) ^ y_lo
    ring_y = jnp.where(home, 1, 0)
    place_far = jnp.where(shift_y == ring_y, 0, 4) + shift_x
    place_own = (place_far + 4) % 8

    size = rows // CHUNKS
    pieces = [lax.slice_in_dim(data, r * size, (r + 1) * size, axis=1) for r in range(CHUNKS)]
    left = z_gather(pieces)

    scaled = scale(data, source_term)
    near = send(scaled, near_y)
    far = send(scaled, far_y)
    far_right = x_gather(jnp.where(home, near, far))
    own_right = x_gather(jnp.where(home, scaled, near))

    mults, sums = [], []
    for r in range(CHUNKS):
        other = send(product(place_far, left[r], far_right), y_across)
        own = product(place_own, left[r], own_right)
        mult, part = combine(own, other, pieces[r])
        mults.append(mult)
        sums.append(part)

    sums = jnp.concatenate(sums, axis=0)
    count = sums.shape[0]
    along_src = [(i, i + 1) for i in range(15)]
    against_src = [(i + 1, i) for i in range(15)]
    above = lax.ppermute(sums[count - 4 :], "src", along_src)
    below = lax.ppermute(sums[:4], "src", against_src)
    tall = jnp.concatenate([above, sums, below], axis=0)
    window = tall[:count] + tall[4 : 4 + count] + tall[8:]
    left_window = lax.ppermute(window, "rcv", along_src)
    right_window = lax.ppermute(window, "rcv", against_src)
    return apply(mults, window, left_window, right_window)


def solution(mesh):
    in_specs = (P(None, "src", "rcv"), P(None, "src"))
    out_specs = P(None, "src", "rcv")
    return jax.shard_map(
        on_device, mesh=mesh, in_specs=in_specs, out_specs=out_specs, check_vma=False
    )
```

```python
import functools

import jax
import jax.numpy as jnp
from jax import lax
from jax.experimental import pallas as pl
from jax.experimental.pallas import tpu as pltpu
from jax.sharding import PartitionSpec as P


LINE = 64
STABILISER = 1e-05
AXES = ("src", "rcv")
NX, NY, NZ = 4, 4, 8
CUTS = (0, 192, 384)
PARTIAL = jnp.bfloat16
VMEM = pl.BlockSpec(memory_space=pltpu.VMEM)
SMEM = pl.BlockSpec(memory_space=pltpu.SMEM)
ANY = pl.BlockSpec(memory_space=pl.ANY)


def linear(x, y, z, core):
    return ((x * 2 + y % 2) * 2 + core) * 16 + z * 2 + y // 2


def send(value, target):
    pairs = []
    for x in range(NX):
        for y in range(NY):
            for z in range(NZ):
                for core in range(2):
                    to = target(x, y, z, core)
                    if to is not None:
                        pairs.append((linear(x, y, z, core), linear(to[0] % NX, to[1] % NY, to[2] % NZ, to[3])))
    return lax.ppermute(value, AXES, pairs)


def z_up(x, y, z, core):
    return x, y, z + 1, core


def z_down(x, y, z, core):
    return x, y, z - 1, core


def x_apart(x, y, z, core):
    return x + 1 - 2 * core, y, z, core


def home_to_opposite(x, y, z, core):
    return (x + 2, y, z, core) if core == y // 2 else None


def away_to_opposite(x, y, z, core):
    return (x + 2, y, z, core) if core != y // 2 else None


def swap_core(x, y, z, core):
    return x, y, z, 1 - core


def y_across(x, y, z, core):
    return x, y + 2, z, core


def near_y(x, y, z, core):
    if y // 2 == core:
        return x, y ^ 1, z, 1 - core
    return x, 3 - y, z, core


def far_y(x, y, z, core):
    if y // 2 == core:
        return None
    return x, y ^ 2, z, 1 - core


def next_src(x, y, z, core):
    src = (x * 2 + y % 2) * 2 + core + (1 if core else -1)
    if not 0 <= src < 16:
        return None
    return src // 4, y // 2 * 2 + src // 2 % 2, z, src % 2


def next_rcv(x, y, z, core):
    rcv = z * 2 + y // 2 + (1 if y // 2 else -1)
    if not 0 <= rcv < 16:
        return None
    return x, rcv % 2 * 2 + y % 2, rcv // 2, core


def kernel_call(kernel, out_shape, in_specs, out_specs, args, flops=0, moved=0, scratch=(), limit=8):
    return pl.pallas_call(
        kernel,
        out_shape=out_shape,
        in_specs=in_specs,
        out_specs=out_specs,
        scratch_shapes=scratch,
        compiler_params=pltpu.CompilerParams(vmem_limit_bytes=limit << 20),
        cost_estimate=pl.CostEstimate(flops=flops, bytes_accessed=moved, transcendentals=0),
    )(*args)


def scale_kernel(data_ref, source_ref, out_ref):
    weights = jnp.transpose(jnp.concatenate([source_ref[...]] * 4, axis=0))
    weight_re = weights[:, 0:1]
    weight_im = weights[:, 1:2]
    recorded_re = data_ref[0].astype(jnp.float32)
    recorded_im = data_ref[1].astype(jnp.float32)
    width = recorded_re.shape[1]
    out_ref[:, :width] = (weight_re * recorded_re - weight_im * recorded_im).astype(jnp.bfloat16)
    out_ref[:, width:] = (weight_re * recorded_im + weight_im * recorded_re).astype(jnp.bfloat16)


def scale(data, source_term):
    _, rows, cols = data.shape
    return kernel_call(
        scale_kernel,
        jax.ShapeDtypeStruct((rows, 2 * cols), jnp.bfloat16),
        [VMEM] * 2,
        VMEM,
        (data, source_term),
        6 * rows * cols,
        8 * rows * cols,
    )


def product_kernel(place_ref, *refs, count):
    left = refs[:8]
    right = refs[8 : 8 + count]
    out_ref, held, panel, total, left_sems, right_sems = refs[8 + count :]
    home = place_ref[18] == 1
    rows, depth = left[0].shape[1], left[0].shape[2]
    for e in range(8):
        s = place_ref[e]
        pltpu.make_async_copy(left[e], held.at[s], left_sems.at[s]).start()
    for s in range(8):
        copy = pltpu.make_async_copy(right[s], panel.at[s], right_sems.at[s])
        if s + 8 < count:
            pl.when(home)(copy.start)
            pl.when(jnp.logical_not(home))(pltpu.make_async_copy(right[s + 8], panel.at[s], right_sems.at[s]).start)
        else:
            copy.start()
    for s in range(0, 8, 2):
        for t in (s, s + 1):
            pltpu.make_async_copy(left[0], held.at[t], left_sems.at[t]).wait()
            pltpu.make_async_copy(right[t], panel.at[t], right_sems.at[t]).wait()
        part = jnp.dot(
            jnp.concatenate([held[s].reshape(2 * rows, depth), held[s + 1].reshape(2 * rows, depth)], axis=1),
            panel[s : s + 2].reshape(2 * depth, panel.shape[2]),
            preferred_element_type=jnp.float32,
        )
        if s == 0:
            total[...] = part
        else:
            total[...] += part
    cols = out_ref.shape[2]
    out_ref[0] = (total[:rows, :cols] - total[rows:, cols:]).astype(out_ref.dtype)
    out_ref[1] = (total[:rows, cols:] + total[rows:, :cols]).astype(out_ref.dtype)


def product(place, left, right, dtype):
    _, rows, depth = left[0].shape
    wide = right[0].shape[1]
    count = len(right)
    return kernel_call(
        functools.partial(product_kernel, count=count),
        jax.ShapeDtypeStruct((2, rows, wide // 2), dtype),
        [SMEM] + [ANY] * (8 + count),
        VMEM,
        (place, *[left[e] for e in range(8)], *right),
        32 * rows * depth * wide,
        16 * (2 * rows + wide) * depth,
        [
            pltpu.VMEM((8, 2, rows, depth), jnp.bfloat16),
            pltpu.VMEM((8, depth, wide), jnp.bfloat16),
            pltpu.VMEM((2 * rows, wide), jnp.float32),
            pltpu.SemaphoreType.DMA((8,)),
            pltpu.SemaphoreType.DMA((8,)),
        ],
        16,
    )


def combine_kernel(place_ref, own_ref, other_ref, data_ref, *refs, ahead):
    if ahead:
        ahead_ref, mult_ref, sums_ref, mate_ref, next_ref = refs
        start = ahead_ref.shape[0]
        sums_ref[:start] = ahead_ref[...]
    else:
        mult_ref, sums_ref = refs
        start = 0
    mult_re = (own_ref[0] + other_ref[0].astype(jnp.float32)).astype(jnp.bfloat16)
    mult_im = (own_ref[1] + other_ref[1].astype(jnp.float32)).astype(jnp.bfloat16)
    mult_ref[0] = mult_re
    mult_ref[1] = mult_im
    rows, cols = mult_re.shape
    lane = lax.broadcasted_iota(jnp.int32, (1, cols), 1) // LINE
    slot = lax.broadcasted_iota(jnp.int32, (1, 128), 1)
    for i in range(rows // LINE):
        span = slice(i * LINE, (i + 1) * LINE)
        m_re = mult_re[span].astype(jnp.float32)
        m_im = mult_im[span].astype(jnp.float32)
        d_re = data_ref[0, span].astype(jnp.float32)
        d_im = data_ref[1, span].astype(jnp.float32)
        terms = (m_re * d_re + m_im * d_im, m_re * d_im - m_im * d_re, m_re * m_re + m_im * m_im)
        along = jnp.concatenate(
            [jnp.sum(term, axis=0, keepdims=True) for term in terms] + [jnp.zeros((1, cols), jnp.float32)], axis=0
        )
        part = jnp.zeros((4, 128), jnp.float32)
        for j in range(cols // LINE):
            block = jnp.sum(jnp.where(lane == j, along, 0.0), axis=1, keepdims=True)
            part = jnp.where(slot == j, block, part)
        sums_ref[pl.ds(start + 4 * i, 4), :] = part
    if ahead:
        upper = place_ref[16] == 0
        first, last = sums_ref[:4, :], sums_ref[sums_ref.shape[0] - 4 :, :]
        mate_ref[...] = jnp.where(upper, last, first)
        next_ref[...] = jnp.where(upper, first, last)


def combine(place, own, other, data, ahead=None):
    _, rows, cols = own.shape
    count = 4 * (rows // LINE)
    args = (place, own, other, data)
    out_shape = [jax.ShapeDtypeStruct((2, rows, cols), jnp.bfloat16)]
    if ahead is None:
        out_shape += [jax.ShapeDtypeStruct((count, 128), jnp.float32)]
    else:
        args += (ahead,)
        out_shape += [jax.ShapeDtypeStruct((count + ahead.shape[0], 128), jnp.float32)]
        out_shape += [jax.ShapeDtypeStruct((4, 128), jnp.float32)] * 2
    return kernel_call(
        functools.partial(combine_kernel, ahead=ahead is not None),
        out_shape,
        [SMEM] + [VMEM] * (len(args) - 1),
        [VMEM] * len(out_shape),
        args,
        16 * rows * cols,
        24 * rows * cols,
    )


def window_kernel(place_ref, sums_ref, mate_ref, next_ref, out_ref):
    upper = place_ref[16] == 0
    mate, other = mate_ref[...], next_ref[...]
    above = jnp.where(upper, other, mate)
    below = jnp.where(upper, mate, other)
    sums = sums_ref[...]
    count = sums.shape[0]
    out_ref[...] = (
        jnp.concatenate([above, sums[: count - 4]], axis=0) + sums + jnp.concatenate([sums[4:], below], axis=0)
    )


def apply_kernel(place_ref, *refs):
    chunks = len(CUTS) - 1
    mults = refs[:chunks]
    window_ref, across_ref, next_ref, out_ref = refs[chunks:]
    lower = place_ref[17] == 0
    across, other = across_ref[...], next_ref[...]
    left = jnp.where(lower, other, across)
    right = jnp.where(lower, across, other)
    window = window_ref[...]
    slot = lax.broadcasted_iota(jnp.int32, window.shape, 1)
    cols = out_ref.shape[2]
    last = cols // LINE - 1
    before = jnp.where(slot == 0, pltpu.roll(left, 128 - last, 1), pltpu.roll(window, 1, 1))
    after = jnp.where(slot == last, pltpu.roll(right, last, 1), pltpu.roll(window, 127, 1))
    window = window + before + after
    lane = lax.broadcasted_iota(jnp.int32, (1, cols), 1) // LINE
    for i in range(CUTS[-1] // LINE):
        energy = window[4 * i + 2 : 4 * i + 3] + STABILISER
        value = window[4 * i : 4 * i + 2] / energy
        spread = jnp.zeros((2, cols), jnp.float32)
        for j in range(last + 1):
            spread = jnp.where(lane == j, value[:, j : j + 1], spread)
        coef_re, coef_im = spread[0:1], spread[1:2]
        r = max(k for k in range(chunks) if CUTS[k] <= i * LINE)
        span = pl.ds(i * LINE - CUTS[r], LINE)
        m_re = mults[r][0, span].astype(jnp.float32)
        m_im = mults[r][1, span].astype(jnp.float32)
        out_ref[0, pl.ds(i * LINE, LINE)] = (coef_re * m_re - coef_im * m_im).astype(jnp.bfloat16)
        out_ref[1, pl.ds(i * LINE, LINE)] = (coef_re * m_im + coef_im * m_re).astype(jnp.bfloat16)


def on_device(data, source_term):
    src = lax.axis_index("src")
    rcv = lax.axis_index("rcv")
    x, y_lo, core = src // 4, (src // 2) % 2, src % 2
    z, y_hi = rcv // 2, rcv % 2
    home = core == y_hi
    block = (z - jnp.arange(8, dtype=jnp.int32)) % 8
    shift_x = (x - block // 2) % 4
    shift_x = jnp.where(core == 0, shift_x, (4 - shift_x) % 4)
    shift_y = (block % 2) ^ y_lo
    ring_y = jnp.where(home, 1, 0)
    flags = jnp.stack([core, y_hi, jnp.where(home, 1, 0)])
    pad = jnp.zeros(8, jnp.int32)
    place_far = jnp.concatenate([jnp.where(shift_y == ring_y, 0, 4) + shift_x, pad, flags])
    own_slot = jnp.where(shift_x == 2, shift_y, 2 + 3 * shift_y + jnp.minimum(shift_x, 2))
    place_own = jnp.concatenate([own_slot, pad, flags])
    place = place_own

    pieces = [data[:, CUTS[r] : CUTS[r + 1]] for r in range(2)]
    left = [{0: piece} for piece in pieces]
    up = list(pieces)
    down = list(pieces)
    for step in range(1, 5):
        for r in range(2):
            if step < 4 or r == 0:
                up[r] = send(up[r], z_up)
                left[r][step] = up[r]
            if step < 4 or r == 1:
                down[r] = send(down[r], z_down)
                left[r][8 - step] = down[r]

    scaled = scale(data, source_term)
    near = send(scaled, near_y)
    far = send(scaled, far_y)

    hs = send(scaled, swap_core)
    h = jnp.where(home, scaled, hs)
    h1 = send(h, x_apart)
    h2 = send(scaled, home_to_opposite)
    h1s = send(h1, swap_core)
    h2s = send(h2, swap_core)

    f = jnp.where(home, near, far)
    fs = send(f, swap_core)
    f1a = send(f, x_apart)
    f1b = send(fs, x_apart)
    f2 = send(f1a, x_apart)
    f1as = send(f1a, swap_core)
    f1bs = send(f1b, swap_core)
    f2s = send(f2, swap_core)
    far_right = [f, f1a, f2, f1bs, fs, f1b, f2s, f1as]

    near, f1a = lax.optimization_barrier((near, f1a))
    ns = send(near, swap_core)
    n = jnp.where(home, ns, near)
    n1 = send(n, x_apart)
    n2 = send(near, away_to_opposite)
    n1s = send(n1, swap_core)
    n2s = send(n2, swap_core)
    own_right = [h2, n2s, h, h1, h1s, n, n1, n1s]
    own_right += [h2s, n2]

    part0 = product(place_far, left[0], far_right, PARTIAL)
    other0 = send(part0, y_across)
    part1 = product(place_far, left[1], far_right, PARTIAL)
    other1 = send(part1, y_across)
    own0 = product(place_own, left[0], own_right, jnp.float32)
    own1 = product(place_own, left[1], own_right, jnp.float32)

    mult0, sums = combine(place, own0, other0, pieces[0])
    mult1, sums, to_mate, to_next = combine(place, own1, other1, pieces[1], sums)
    from_mate = send(to_mate, swap_core)
    from_next = send(to_next, next_src)
    window = kernel_call(
        window_kernel,
        jax.ShapeDtypeStruct(sums.shape, jnp.float32),
        [SMEM] + [VMEM] * 3,
        VMEM,
        (place, sums, from_mate, from_next),
    )
    from_across = send(window, y_across)
    from_next = send(window, next_rcv)
    return kernel_call(
        apply_kernel,
        jax.ShapeDtypeStruct(data.shape, jnp.bfloat16),
        [SMEM] + [VMEM] * 5,
        VMEM,
        (place, mult0, mult1, window, from_across, from_next),
        12 * data.shape[1] * data.shape[2],
        8 * data.shape[1] * data.shape[2],
    )


def solution(mesh):
    in_specs = (P(None, "src", "rcv"), P(None, "src"))
    out_specs = P(None, "src", "rcv")
    return jax.shard_map(
        on_device, mesh=mesh, in_specs=in_specs, out_specs=out_specs, check_vma=False
    )
```

```python
import functools

import jax
import jax.numpy as jnp
from jax import lax
from jax.experimental import pallas as pl
from jax.experimental.pallas import tpu as pltpu
from jax.sharding import PartitionSpec as P


LINE = 64
STABILISER = 1e-05
AXES = ("src", "rcv")
NX, NY, NZ = 4, 4, 8
CUTS = (0, 192, 384)
PARTIAL = jnp.bfloat16
VMEM = pl.BlockSpec(memory_space=pltpu.VMEM)
SMEM = pl.BlockSpec(memory_space=pltpu.SMEM)
ANY = pl.BlockSpec(memory_space=pl.ANY)


def linear(x, y, z, core):
    return ((x * 2 + y % 2) * 2 + core) * 16 + z * 2 + y // 2


def send(value, target):
    pairs = []
    for x in range(NX):
        for y in range(NY):
            for z in range(NZ):
                for core in range(2):
                    to = target(x, y, z, core)
                    if to is not None:
                        pairs.append((linear(x, y, z, core), linear(to[0] % NX, to[1] % NY, to[2] % NZ, to[3])))
    return lax.ppermute(value, AXES, pairs)


def z_up(x, y, z, core):
    return x, y, z + 1, core


def z_down(x, y, z, core):
    return x, y, z - 1, core


def x_apart(x, y, z, core):
    return x + 1 - 2 * core, y, z, core


def home_to_opposite(x, y, z, core):
    return (x + 2, y, z, core) if core == y // 2 else None


def away_to_opposite(x, y, z, core):
    return (x + 2, y, z, core) if core != y // 2 else None


def swap_core(x, y, z, core):
    return x, y, z, 1 - core


def y_across(x, y, z, core):
    return x, y + 2, z, core


def near_y(x, y, z, core):
    if y // 2 == core:
        return x, y ^ 1, z, 1 - core
    return x, 3 - y, z, core


def far_y(x, y, z, core):
    if y // 2 == core:
        return None
    return x, y ^ 2, z, 1 - core


def next_src(x, y, z, core):
    src = (x * 2 + y % 2) * 2 + core + (1 if core else -1)
    if not 0 <= src < 16:
        return None
    return src // 4, y // 2 * 2 + src // 2 % 2, z, src % 2


def next_rcv(x, y, z, core):
    rcv = z * 2 + y // 2 + (1 if y // 2 else -1)
    if not 0 <= rcv < 16:
        return None
    return x, rcv % 2 * 2 + y % 2, rcv // 2, core


def kernel_call(kernel, out_shape, in_specs, out_specs, args, flops=0, moved=0, scratch=(), limit=8):
    return pl.pallas_call(
        kernel,
        out_shape=out_shape,
        in_specs=in_specs,
        out_specs=out_specs,
        scratch_shapes=scratch,
        compiler_params=pltpu.CompilerParams(vmem_limit_bytes=limit << 20),
        cost_estimate=pl.CostEstimate(flops=flops, bytes_accessed=moved, transcendentals=0),
    )(*args)


def scale_kernel(data_ref, source_ref, out_ref):
    weights = jnp.transpose(jnp.concatenate([source_ref[...]] * 4, axis=0))
    weight_re = weights[:, 0:1]
    weight_im = weights[:, 1:2]
    recorded_re = data_ref[0].astype(jnp.float32)
    recorded_im = data_ref[1].astype(jnp.float32)
    width = recorded_re.shape[1]
    out_ref[:, :width] = (weight_re * recorded_re - weight_im * recorded_im).astype(jnp.bfloat16)
    out_ref[:, width:] = (weight_re * recorded_im + weight_im * recorded_re).astype(jnp.bfloat16)


def scale(data, source_term):
    _, rows, cols = data.shape
    return kernel_call(
        scale_kernel,
        jax.ShapeDtypeStruct((rows, 2 * cols), jnp.bfloat16),
        [VMEM] * 2,
        VMEM,
        (data, source_term),
        6 * rows * cols,
        8 * rows * cols,
    )


def place_kernel(out_ref):
    src = lax.axis_index("src")
    rcv = lax.axis_index("rcv")
    x, y_lo, core = src >> 2, (src >> 1) & 1, src & 1
    z, y_hi = rcv >> 1, rcv & 1
    home = jnp.where(core == y_hi, 1, 0)
    for e in range(8):
        block = (z - e) & 7
        shift_x = (x - (block >> 1)) & 3
        shift_x = jnp.where(core == 0, shift_x, (4 - shift_x) & 3)
        shift_y = (block & 1) ^ y_lo
        out_ref[e] = jnp.where(shift_y == home, 0, 4) + shift_x
        out_ref[8 + e] = jnp.where(shift_x == 2, shift_y, 2 + 3 * shift_y + jnp.minimum(shift_x, 2))
    out_ref[16] = core
    out_ref[17] = y_hi
    out_ref[18] = home


def find_place():
    return pl.pallas_call(
        place_kernel, out_shape=jax.ShapeDtypeStruct((19,), jnp.int32), out_specs=SMEM, name="k_place"
    )()


def pick_kernel(place_ref, at_home_ref, away_ref, out_ref):
    out_ref[...] = jnp.where(place_ref[18] == 1, at_home_ref[...], away_ref[...])


def pick(place, at_home, away):
    return kernel_call(
        pick_kernel,
        jax.ShapeDtypeStruct(away.shape, away.dtype),
        [SMEM, VMEM, VMEM],
        VMEM,
        (place, at_home, away),
        0,
        6 * away.size,
    )


def product_kernel(place_ref, *refs, count, base):
    left = refs[:8]
    right = refs[8 : 8 + count]
    out_ref, held, total = refs[8 + count :]
    home = place_ref[18] == 1
    rows, depth = left[0].shape[1], left[0].shape[2]
    for e in range(8):
        held[place_ref[base + e]] = left[e][...]

    def panel(s):
        if s + 8 < count:
            return jnp.where(home, right[s][...], right[s + 8][...])
        return right[s][...]

    for s in range(0, 8, 2):
        part = jnp.dot(
            jnp.concatenate([held[s].reshape(2 * rows, depth), held[s + 1].reshape(2 * rows, depth)], axis=1),
            jnp.concatenate([panel(s), panel(s + 1)], axis=0),
            preferred_element_type=jnp.float32,
        )
        if s == 0:
            total[...] = part
        else:
            total[...] += part
    cols = out_ref.shape[2]
    out_ref[0] = (total[:rows, :cols] - total[rows:, cols:]).astype(out_ref.dtype)
    out_ref[1] = (total[:rows, cols:] + total[rows:, :cols]).astype(out_ref.dtype)


def product(place, base, left, right, dtype):
    _, rows, depth = left[0].shape
    wide = right[0].shape[1]
    count = len(right)
    return kernel_call(
        functools.partial(product_kernel, count=count, base=base),
        jax.ShapeDtypeStruct((2, rows, wide // 2), dtype),
        [SMEM] + [VMEM] * (8 + count),
        VMEM,
        (place, *[left[e] for e in range(8)], *right),
        32 * rows * depth * wide,
        16 * (2 * rows + wide) * depth,
        [
            pltpu.VMEM((8, 2, rows, depth), jnp.bfloat16),
            pltpu.VMEM((2 * rows, wide), jnp.float32),
        ],
        16,
    )


def combine_kernel(place_ref, own_ref, other_ref, data_ref, *refs, ahead):
    if ahead:
        ahead_ref, mult_ref, sums_ref, mate_ref, next_ref = refs
        start = ahead_ref.shape[0]
        sums_ref[:start] = ahead_ref[...]
    else:
        mult_ref, sums_ref = refs
        start = 0
    mult_re = (own_ref[0] + other_ref[0].astype(jnp.float32)).astype(jnp.bfloat16)
    mult_im = (own_ref[1] + other_ref[1].astype(jnp.float32)).astype(jnp.bfloat16)
    mult_ref[0] = mult_re
    mult_ref[1] = mult_im
    rows, cols = mult_re.shape
    lane = lax.broadcasted_iota(jnp.int32, (1, cols), 1) // LINE
    slot = lax.broadcasted_iota(jnp.int32, (1, 128), 1)
    for i in range(rows // LINE):
        span = slice(i * LINE, (i + 1) * LINE)
        m_re = mult_re[span].astype(jnp.float32)
        m_im = mult_im[span].astype(jnp.float32)
        d_re = data_ref[0, span].astype(jnp.float32)
        d_im = data_ref[1, span].astype(jnp.float32)
        terms = (m_re * d_re + m_im * d_im, m_re * d_im - m_im * d_re, m_re * m_re + m_im * m_im)
        along = jnp.concatenate(
            [jnp.sum(term, axis=0, keepdims=True) for term in terms] + [jnp.zeros((1, cols), jnp.float32)], axis=0
        )
        part = jnp.zeros((4, 128), jnp.float32)
        for j in range(cols // LINE):
            block = jnp.sum(jnp.where(lane == j, along, 0.0), axis=1, keepdims=True)
            part = jnp.where(slot == j, block, part)
        sums_ref[pl.ds(start + 4 * i, 4), :] = part
    if ahead:
        upper = place_ref[16] == 0
        first, last = sums_ref[:4, :], sums_ref[sums_ref.shape[0] - 4 :, :]
        mate_ref[...] = jnp.where(upper, last, first)
        next_ref[...] = jnp.where(upper, first, last)


def combine(place, own, other, data, ahead=None):
    _, rows, cols = own.shape
    count = 4 * (rows // LINE)
    args = (place, own, other, data)
    out_shape = [jax.ShapeDtypeStruct((2, rows, cols), jnp.bfloat16)]
    if ahead is None:
        out_shape += [jax.ShapeDtypeStruct((count, 128), jnp.float32)]
    else:
        args += (ahead,)
        out_shape += [jax.ShapeDtypeStruct((count + ahead.shape[0], 128), jnp.float32)]
        out_shape += [jax.ShapeDtypeStruct((4, 128), jnp.float32)] * 2
    return kernel_call(
        functools.partial(combine_kernel, ahead=ahead is not None),
        out_shape,
        [SMEM] + [VMEM] * (len(args) - 1),
        [VMEM] * len(out_shape),
        args,
        16 * rows * cols,
        24 * rows * cols,
    )


def window_kernel(place_ref, sums_ref, mate_ref, next_ref, out_ref):
    upper = place_ref[16] == 0
    mate, other = mate_ref[...], next_ref[...]
    above = jnp.where(upper, other, mate)
    below = jnp.where(upper, mate, other)
    sums = sums_ref[...]
    count = sums.shape[0]
    out_ref[...] = (
        jnp.concatenate([above, sums[: count - 4]], axis=0) + sums + jnp.concatenate([sums[4:], below], axis=0)
    )


def apply_kernel(place_ref, *refs):
    chunks = len(CUTS) - 1
    mults = refs[:chunks]
    window_ref, across_ref, next_ref, out_ref = refs[chunks:]
    lower = place_ref[17] == 0
    across, other = across_ref[...], next_ref[...]
    left = jnp.where(lower, other, across)
    right = jnp.where(lower, across, other)
    window = window_ref[...]
    slot = lax.broadcasted_iota(jnp.int32, window.shape, 1)
    cols = out_ref.shape[2]
    last = cols // LINE - 1
    before = jnp.where(slot == 0, pltpu.roll(left, 128 - last, 1), pltpu.roll(window, 1, 1))
    after = jnp.where(slot == last, pltpu.roll(right, last, 1), pltpu.roll(window, 127, 1))
    window = window + before + after
    lane = lax.broadcasted_iota(jnp.int32, (1, cols), 1) // LINE
    for i in range(CUTS[-1] // LINE):
        energy = window[4 * i + 2 : 4 * i + 3] + STABILISER
        value = window[4 * i : 4 * i + 2] / energy
        spread = jnp.zeros((2, cols), jnp.float32)
        for j in range(last + 1):
            spread = jnp.where(lane == j, value[:, j : j + 1], spread)
        coef_re, coef_im = spread[0:1], spread[1:2]
        r = max(k for k in range(chunks) if CUTS[k] <= i * LINE)
        span = pl.ds(i * LINE - CUTS[r], LINE)
        m_re = mults[r][0, span].astype(jnp.float32)
        m_im = mults[r][1, span].astype(jnp.float32)
        out_ref[0, pl.ds(i * LINE, LINE)] = (coef_re * m_re - coef_im * m_im).astype(jnp.bfloat16)
        out_ref[1, pl.ds(i * LINE, LINE)] = (coef_re * m_im + coef_im * m_re).astype(jnp.bfloat16)


def on_device(data, source_term):
    place = find_place()
    pieces = [data[:, CUTS[r] : CUTS[r + 1]] for r in range(2)]
    left = [{0: piece} for piece in pieces]
    up = list(pieces)
    down = list(pieces)
    for step in range(1, 5):
        for r in range(2):
            if step < 4 or r == 0:
                up[r] = send(up[r], z_up)
                left[r][step] = up[r]
            if step < 4 or r == 1:
                down[r] = send(down[r], z_down)
                left[r][8 - step] = down[r]

    scaled = scale(data, source_term)
    near = send(scaled, near_y)
    far = send(scaled, far_y)

    hs = send(scaled, swap_core)
    h = pick(place, scaled, hs)
    h1 = send(h, x_apart)
    h2 = send(scaled, home_to_opposite)
    h1s = send(h1, swap_core)
    h2s = send(h2, swap_core)

    f = pick(place, near, far)
    fs = send(f, swap_core)
    f1a = send(f, x_apart)
    f1b = send(fs, x_apart)
    f2 = send(f1a, x_apart)
    f1as = send(f1a, swap_core)
    f1bs = send(f1b, swap_core)
    f2s = send(f2, swap_core)
    far_right = [f, f1a, f2, f1bs, fs, f1b, f2s, f1as]

    ns = send(near, swap_core)
    n = pick(place, ns, near)
    n1 = send(n, x_apart)
    n2 = send(near, away_to_opposite)
    n1s = send(n1, swap_core)
    n2s = send(n2, swap_core)
    own_right = [h2, n2s, h, h1, h1s, n, n1, n1s]
    own_right += [h2s, n2]

    part0 = product(place, 0, left[0], far_right, PARTIAL)
    other0 = send(part0, y_across)
    part1 = product(place, 0, left[1], far_right, PARTIAL)
    other1 = send(part1, y_across)
    own0 = product(place, 8, left[0], own_right, jnp.float32)
    own1 = product(place, 8, left[1], own_right, jnp.float32)

    mult0, sums = combine(place, own0, other0, pieces[0])
    mult1, sums, to_mate, to_next = combine(place, own1, other1, pieces[1], sums)
    from_mate = send(to_mate, swap_core)
    from_next = send(to_next, next_src)
    window = kernel_call(
        window_kernel,
        jax.ShapeDtypeStruct(sums.shape, jnp.float32),
        [SMEM] + [VMEM] * 3,
        VMEM,
        (place, sums, from_mate, from_next),
    )
    from_across = send(window, y_across)
    from_next = send(window, next_rcv)
    return kernel_call(
        apply_kernel,
        jax.ShapeDtypeStruct(data.shape, jnp.bfloat16),
        [SMEM] + [VMEM] * 5,
        VMEM,
        (place, mult0, mult1, window, from_across, from_next),
        12 * data.shape[1] * data.shape[2],
        8 * data.shape[1] * data.shape[2],
    )


def solution(mesh):
    in_specs = (P(None, "src", "rcv"), P(None, "src"))
    out_specs = P(None, "src", "rcv")
    return jax.shard_map(
        on_device, mesh=mesh, in_specs=in_specs, out_specs=out_specs, check_vma=False
    )
```

```python
import functools

import jax
import jax.numpy as jnp
from jax import lax
from jax.experimental import pallas as pl
from jax.experimental.pallas import tpu as pltpu
from jax.sharding import PartitionSpec as P


LINE = 64
STABILISER = 1e-05
AXES = ("src", "rcv")
NX, NY, NZ = 4, 4, 8
PARTIAL = jnp.bfloat16
VMEM = pl.BlockSpec(memory_space=pltpu.VMEM)
SMEM = pl.BlockSpec(memory_space=pltpu.SMEM)


def linear(x, y, z, core):
    return ((x * 2 + y % 2) * 2 + core) * 16 + z * 2 + y // 2


def send(value, target):
    pairs = []
    for x in range(NX):
        for y in range(NY):
            for z in range(NZ):
                for core in range(2):
                    to = target(x, y, z, core)
                    if to is not None:
                        pairs.append((linear(x, y, z, core), linear(to[0] % NX, to[1] % NY, to[2] % NZ, to[3])))
    return lax.ppermute(value, AXES, pairs)


def z_up(x, y, z, core):
    return x, y, z + 1, core


def z_down(x, y, z, core):
    return x, y, z - 1, core


def x_apart(x, y, z, core):
    return x + 1 - 2 * core, y, z, core


def home_to_opposite(x, y, z, core):
    return (x + 2, y, z, core) if core == y // 2 else None


def away_to_opposite(x, y, z, core):
    return (x + 2, y, z, core) if core != y // 2 else None


def swap_core(x, y, z, core):
    return x, y, z, 1 - core


def y_across(x, y, z, core):
    return x, y + 2, z, core


def near_y(x, y, z, core):
    if y // 2 == core:
        return x, y ^ 1, z, 1 - core
    return x, 3 - y, z, core


def far_y(x, y, z, core):
    if y // 2 == core:
        return None
    return x, y ^ 2, z, 1 - core


def next_src(x, y, z, core):
    src = (x * 2 + y % 2) * 2 + core + (1 if core else -1)
    if not 0 <= src < 16:
        return None
    return src // 4, y // 2 * 2 + src // 2 % 2, z, src % 2


def next_rcv(x, y, z, core):
    rcv = z * 2 + y // 2 + (1 if y // 2 else -1)
    if not 0 <= rcv < 16:
        return None
    return x, rcv % 2 * 2 + y % 2, rcv // 2, core


def kernel_call(kernel, out_shape, in_specs, out_specs, args, flops=0, moved=0, scratch=(), limit=8):
    return pl.pallas_call(
        kernel,
        out_shape=out_shape,
        in_specs=in_specs,
        out_specs=out_specs,
        scratch_shapes=scratch,
        compiler_params=pltpu.CompilerParams(vmem_limit_bytes=limit << 20),
        cost_estimate=pl.CostEstimate(flops=flops, bytes_accessed=moved, transcendentals=0),
    )(*args)


def begin_kernel(data_ref, source_ref, piece0_ref, piece1_ref, scaled_ref):
    core = lax.axis_index("src") & 1
    half = data_ref.shape[1] // 2
    width = data_ref.shape[2]
    first = pl.multiple_of(core * half, half)
    piece0_ref[...] = data_ref[:, pl.ds(first, half)]
    piece1_ref[...] = data_ref[:, pl.ds(pl.multiple_of(half - first, half), half)]
    weights = jnp.transpose(jnp.concatenate([source_ref[...]] * 4, axis=0))
    weight_re = weights[:, 0:1]
    weight_im = weights[:, 1:2]
    recorded_re = data_ref[0].astype(jnp.float32)
    recorded_im = data_ref[1].astype(jnp.float32)
    scaled_ref[:, :width] = (weight_re * recorded_re - weight_im * recorded_im).astype(jnp.bfloat16)
    scaled_ref[:, width:] = (weight_re * recorded_im + weight_im * recorded_re).astype(jnp.bfloat16)


def begin(data, source_term):
    _, rows, cols = data.shape
    piece = jax.ShapeDtypeStruct((2, rows // 2, cols), jnp.bfloat16)
    return kernel_call(
        begin_kernel,
        (piece, piece, jax.ShapeDtypeStruct((rows, 2 * cols), jnp.bfloat16)),
        [VMEM] * 2,
        [VMEM] * 3,
        (data, source_term),
        6 * rows * cols,
        12 * rows * cols,
    )


def place_kernel(out_ref):
    src = lax.axis_index("src")
    rcv = lax.axis_index("rcv")
    x, y_lo, core = src >> 2, (src >> 1) & 1, src & 1
    z, y_hi = rcv >> 1, rcv & 1
    home = jnp.where(core == y_hi, 1, 0)
    for e in range(8):
        block = (z - e) & 7
        shift_x = (x - (block >> 1)) & 3
        shift_x = jnp.where(core == 0, shift_x, (4 - shift_x) & 3)
        shift_y = (block & 1) ^ y_lo
        out_ref[e] = jnp.where(shift_y == home, 0, 4) + shift_x
    for s, (shift_y, shift_x) in enumerate(((0, 2), (1, 2), (0, 0), (0, 1), (0, 3), (1, 0), (1, 1), (1, 3))):
        out_ref[8 + s] = jnp.where(home == shift_y, 0, 4) + shift_x
    out_ref[16] = core
    out_ref[17] = y_hi
    out_ref[18] = home


def find_place():
    return kernel_call(place_kernel, jax.ShapeDtypeStruct((19,), jnp.int32), [], SMEM, ())


def pick_kernel(place_ref, at_home_ref, away_ref, out_ref):
    out_ref[...] = jnp.where(place_ref[18] == 1, at_home_ref[...], away_ref[...])


def pick(place, at_home, away):
    return kernel_call(
        pick_kernel,
        jax.ShapeDtypeStruct(away.shape, away.dtype),
        [SMEM, VMEM, VMEM],
        VMEM,
        (place, at_home, away),
        0,
        6 * away.size,
    )


def product_kernel(place_ref, *refs, fill, slots, base, begun, finish, count):
    left, refs = (refs[:8], refs[8:]) if fill else (None, refs)
    held_ref, refs = (None, refs) if fill else (refs[0], refs[1:])
    first_ref, refs = (refs[0], refs[1:]) if begun else (None, refs)
    right, refs = refs[:count], refs[count:]
    if fill:
        held_ref, refs = refs[0], refs[1:]
        for e in range(8):
            held_ref[place_ref[e]] = left[e][...]
    out_ref = refs[0]
    total = refs[1] if finish else out_ref
    home = place_ref[18] == 1
    rows, depth = held_ref.shape[2], held_ref.shape[3]

    def row_block(s):
        return held_ref[s if base is None else place_ref[base + s]].reshape(2 * rows, depth)

    def panel(i):
        if i == 0 and count > len(slots):
            return jnp.where(home, right[0][...], right[count - 1][...])
        return right[i][...]

    for i in range(0, len(slots), 2):
        part = jnp.dot(
            jnp.concatenate([row_block(slots[i]), row_block(slots[i + 1])], axis=1),
            jnp.concatenate([panel(i), panel(i + 1)], axis=0),
            preferred_element_type=jnp.float32,
        )
        if i > 0:
            total[...] += part
        elif begun:
            total[...] = first_ref[...] + part
        else:
            total[...] = part
    if finish:
        cols = out_ref.shape[2]
        out_ref[0] = (total[:rows, :cols] - total[rows:, cols:]).astype(out_ref.dtype)
        out_ref[1] = (total[:rows, cols:] + total[rows:, :cols]).astype(out_ref.dtype)


def product(place, left, right, slots, base=None, first=None, dtype=None):
    fill = isinstance(left, dict)
    lefts = [left[e] for e in range(8)] if fill else [left]
    rows, depth = lefts[0].shape[-2:]
    wide = right[0].shape[1]
    args = (place, *lefts, *([] if first is None else [first]), *right)
    out_shape = [jax.ShapeDtypeStruct((8, 2, rows, depth), jnp.bfloat16)] if fill else []
    scratch = []
    if dtype is None:
        out_shape.append(jax.ShapeDtypeStruct((2 * rows, wide), jnp.float32))
    else:
        out_shape.append(jax.ShapeDtypeStruct((2, rows, wide // 2), dtype))
        scratch = [pltpu.VMEM((2 * rows, wide), jnp.float32)]
    out = kernel_call(
        functools.partial(
            product_kernel,
            fill=fill,
            slots=slots,
            base=base,
            begun=first is not None,
            finish=dtype is not None,
            count=len(right),
        ),
        out_shape,
        [SMEM] + [VMEM] * (len(args) - 1),
        [VMEM] * len(out_shape),
        args,
        4 * len(slots) * rows * depth * wide,
        2 * len(slots) * (2 * rows + wide) * depth,
        scratch,
        12,
    )
    return out if fill else out[0]


def combine_kernel(place_ref, own_ref, other_ref, data_ref, *refs, last):
    if last:
        ahead_ref, mult_ref, all_ref, edge_ref, sums_ref = refs
    else:
        mult_ref, sums_ref, edge_ref = refs
    mult_re = (own_ref[0] + other_ref[0].astype(jnp.float32)).astype(jnp.bfloat16)
    mult_im = (own_ref[1] + other_ref[1].astype(jnp.float32)).astype(jnp.bfloat16)
    mult_ref[0] = mult_re
    mult_ref[1] = mult_im
    rows, cols = mult_re.shape
    lane = lax.broadcasted_iota(jnp.int32, (1, cols), 1) // LINE
    slot = lax.broadcasted_iota(jnp.int32, (1, 128), 1)
    for i in range(rows // LINE):
        span = slice(i * LINE, (i + 1) * LINE)
        m_re = mult_re[span].astype(jnp.float32)
        m_im = mult_im[span].astype(jnp.float32)
        d_re = data_ref[0, span].astype(jnp.float32)
        d_im = data_ref[1, span].astype(jnp.float32)
        terms = (m_re * d_re + m_im * d_im, m_re * d_im - m_im * d_re, m_re * m_re + m_im * m_im)
        along = jnp.concatenate(
            [jnp.sum(term, axis=0, keepdims=True) for term in terms] + [jnp.zeros((1, cols), jnp.float32)], axis=0
        )
        part = jnp.zeros((4, 128), jnp.float32)
        for j in range(cols // LINE):
            block = jnp.sum(jnp.where(lane == j, along, 0.0), axis=1, keepdims=True)
            part = jnp.where(slot == j, block, part)
        sums_ref[pl.ds(4 * i, 4), :] = part
    upper = place_ref[16] == 0
    count = sums_ref.shape[0]
    if last:
        all_ref[:count] = jnp.where(upper, ahead_ref[...], sums_ref[...])
        all_ref[count:] = jnp.where(upper, sums_ref[...], ahead_ref[...])
        edge_ref[...] = jnp.where(upper, sums_ref[count - 4 :], sums_ref[:4])
    else:
        edge_ref[...] = jnp.where(upper, sums_ref[:4], sums_ref[count - 4 :])


def combine(place, own, other, data, ahead=None):
    _, rows, cols = own.shape
    count = 4 * (rows // LINE)
    args = (place, own, other, data)
    mult = jax.ShapeDtypeStruct((2, rows, cols), jnp.bfloat16)
    sums = jax.ShapeDtypeStruct((count, 128), jnp.float32)
    edge = jax.ShapeDtypeStruct((4, 128), jnp.float32)
    if ahead is None:
        out_shape = [mult, sums, edge]
        scratch = []
    else:
        args += (ahead,)
        out_shape = [mult, jax.ShapeDtypeStruct((2 * count, 128), jnp.float32), edge]
        scratch = [pltpu.VMEM((count, 128), jnp.float32)]
    return kernel_call(
        functools.partial(combine_kernel, last=ahead is not None),
        out_shape,
        [SMEM] + [VMEM] * (len(args) - 1),
        [VMEM] * 3,
        args,
        16 * rows * cols,
        24 * rows * cols,
        scratch,
    )


def window_kernel(place_ref, sums_ref, mate_ref, next_ref, out_ref):
    upper = place_ref[16] == 0
    mate, other = mate_ref[...], next_ref[...]
    above = jnp.where(upper, other, mate)
    below = jnp.where(upper, mate, other)
    sums = sums_ref[...]
    count = sums.shape[0]
    out_ref[...] = (
        jnp.concatenate([above, sums[: count - 4]], axis=0) + sums + jnp.concatenate([sums[4:], below], axis=0)
    )


def apply_kernel(place_ref, *refs):
    mults = refs[:2]
    window_ref, across_ref, next_ref, out_ref = refs[2:]
    lower = place_ref[17] == 0
    across, other = across_ref[...], next_ref[...]
    left = jnp.where(lower, other, across)
    right = jnp.where(lower, across, other)
    window = window_ref[...]
    slot = lax.broadcasted_iota(jnp.int32, window.shape, 1)
    cols = out_ref.shape[2]
    last = cols // LINE - 1
    before = jnp.where(slot == 0, pltpu.roll(left, 128 - last, 1), pltpu.roll(window, 1, 1))
    after = jnp.where(slot == last, pltpu.roll(right, last, 1), pltpu.roll(window, 127, 1))
    window = window + before + after
    lane = lax.broadcasted_iota(jnp.int32, (1, cols), 1) // LINE
    core = place_ref[16]
    half = window.shape[0] // 2
    rows = mults[0].shape[1]
    for r, mult_ref in enumerate(mults):
        chunk = jnp.where(core == r, window[:half], window[half:])
        start = jnp.where(core == r, 0, rows)
        for i in range(rows // LINE):
            energy = chunk[4 * i + 2 : 4 * i + 3] + STABILISER
            value = chunk[4 * i : 4 * i + 2] / energy
            spread = jnp.zeros((2, cols), jnp.float32)
            for j in range(last + 1):
                spread = jnp.where(lane == j, value[:, j : j + 1], spread)
            coef_re, coef_im = spread[0:1], spread[1:2]
            span = pl.ds(i * LINE, LINE)
            m_re = mult_ref[0, span].astype(jnp.float32)
            m_im = mult_ref[1, span].astype(jnp.float32)
            into = pl.ds(pl.multiple_of(start + i * LINE, LINE), LINE)
            out_ref[0, into] = (coef_re * m_re - coef_im * m_im).astype(jnp.bfloat16)
            out_ref[1, into] = (coef_re * m_im + coef_im * m_re).astype(jnp.bfloat16)


def on_device(data, source_term):
    place = find_place()
    piece0, piece1, scaled = begin(data, source_term)
    pieces = [piece0, piece1]
    left = [{0: piece} for piece in pieces]
    up = list(pieces)
    down = list(pieces)
    for step in range(1, 5):
        for r in range(2):
            if step < 4 or r == 0:
                up[r] = send(up[r], z_up)
                left[r][step] = up[r]
            if step < 4 or r == 1:
                down[r] = send(down[r], z_down)
                left[r][8 - step] = down[r]

    near = send(scaled, near_y)
    far = send(scaled, far_y)

    hs = send(scaled, swap_core)
    h = pick(place, scaled, hs)
    h1 = send(h, x_apart)
    h2 = send(scaled, home_to_opposite)
    h1s = send(h1, swap_core)
    h2s = send(h2, swap_core)

    f = pick(place, near, far)
    fs = send(f, swap_core)
    f1a = send(f, x_apart)
    f1b = send(fs, x_apart)
    f2 = send(f1a, x_apart)
    f1as = send(f1a, swap_core)
    f1bs = send(f1b, swap_core)
    f2s = send(f2, swap_core)

    ns = send(near, swap_core)
    n = pick(place, ns, near)
    n1 = send(n, x_apart)
    n2 = send(near, away_to_opposite)
    n1s = send(n1, swap_core)
    n2s = send(n2, swap_core)

    held0, part = product(place, left[0], [f, f1a, f1bs, fs, f1b, f1as], (0, 1, 3, 4, 5, 7))
    part = product(place, held0, [f2, f2s], (2, 6), None, part, PARTIAL)
    other0 = send(part, y_across)
    every = [f, f1a, f2, f1bs, fs, f1b, f2s, f1as]
    held1, part = product(place, left[1], every, tuple(range(8)), None, None, PARTIAL)
    other1 = send(part, y_across)
    own0 = product(place, held0, [h2, h, h1, h1s, h2s], (0, 2, 3, 4), 8)
    own1 = product(place, held1, [h2, h, h1, h1s, h2s], (0, 2, 3, 4), 8)
    own0 = product(place, held0, [n2s, n, n1, n1s, n2], (1, 5, 6, 7), 8, own0, jnp.float32)
    own1 = product(place, held1, [n2s, n, n1, n1s, n2], (1, 5, 6, 7), 8, own1, jnp.float32)

    mult0, sums, edge = combine(place, own0, other0, pieces[0])
    from_next = send(edge, next_src)
    mult1, sums, edge = combine(place, own1, other1, pieces[1], sums)
    from_mate = send(edge, swap_core)
    window = kernel_call(
        window_kernel,
        jax.ShapeDtypeStruct(sums.shape, jnp.float32),
        [SMEM] + [VMEM] * 3,
        VMEM,
        (place, sums, from_mate, from_next),
    )
    from_across = send(window, y_across)
    from_next = send(window, next_rcv)
    return kernel_call(
        apply_kernel,
        jax.ShapeDtypeStruct(data.shape, jnp.bfloat16),
        [SMEM] + [VMEM] * 5,
        VMEM,
        (place, mult0, mult1, window, from_across, from_next),
        12 * data.shape[1] * data.shape[2],
        8 * data.shape[1] * data.shape[2],
    )


def solution(mesh):
    in_specs = (P(None, "src", "rcv"), P(None, "src"))
    out_specs = P(None, "src", "rcv")
    return jax.shard_map(on_device, mesh=mesh, in_specs=in_specs, out_specs=out_specs, check_vma=False)
```

```python
import functools

import jax
import jax.numpy as jnp
from jax import lax
from jax.experimental import pallas as pl
from jax.experimental.pallas import tpu as pltpu
from jax.sharding import PartitionSpec as P


LINE = 64
STABILISER = 1e-05
AXES = ("src", "rcv")
NX, NY, NZ = 4, 4, 8
PARTIAL = jnp.bfloat16
VMEM = pl.BlockSpec(memory_space=pltpu.VMEM)
SMEM = pl.BlockSpec(memory_space=pltpu.SMEM)


def linear(x, y, z, core):
    return ((x * 2 + y % 2) * 2 + core) * 16 + z * 2 + y // 2


def send(value, target):
    pairs = []
    for x in range(NX):
        for y in range(NY):
            for z in range(NZ):
                for core in range(2):
                    to = target(x, y, z, core)
                    if to is not None:
                        pairs.append((linear(x, y, z, core), linear(to[0] % NX, to[1] % NY, to[2] % NZ, to[3])))
    return lax.ppermute(value, AXES, pairs)


def z_up(x, y, z, core):
    return x, y, z + 1, core


def z_down(x, y, z, core):
    return x, y, z - 1, core


def x_apart(x, y, z, core):
    return x + 1 - 2 * core, y, z, core


def home_to_opposite(x, y, z, core):
    return (x + 2, y, z, core) if core == y // 2 else None


def swap_core(x, y, z, core):
    return x, y, z, 1 - core


def y_across(x, y, z, core):
    return x, y + 2, z, core


def near_y(x, y, z, core):
    if y // 2 == core:
        return None
    return x, 3 - y, z, core


def y_beside(x, y, z, core):
    return x, y ^ 1, z, core


def far_y(x, y, z, core):
    if y // 2 == core:
        return None
    return x, y ^ 2, z, 1 - core


def next_src(x, y, z, core):
    src = (x * 2 + y % 2) * 2 + core + (1 if core else -1)
    if not 0 <= src < 16:
        return None
    return src // 4, y // 2 * 2 + src // 2 % 2, z, src % 2


def next_rcv(x, y, z, core):
    rcv = z * 2 + y // 2 + (1 if y // 2 else -1)
    if not 0 <= rcv < 16:
        return None
    return x, rcv % 2 * 2 + y % 2, rcv // 2, core


def kernel_call(kernel, out_shape, in_specs, out_specs, args, flops=0, moved=0, scratch=(), limit=8):
    return pl.pallas_call(
        kernel,
        out_shape=out_shape,
        in_specs=in_specs,
        out_specs=out_specs,
        scratch_shapes=scratch,
        compiler_params=pltpu.CompilerParams(vmem_limit_bytes=limit << 20),
        cost_estimate=pl.CostEstimate(flops=flops, bytes_accessed=moved, transcendentals=0),
    )(*args)


def begin_kernel(data_ref, source_ref, piece0_ref, piece1_ref, scaled_ref):
    core = lax.axis_index("src") & 1
    half = data_ref.shape[1] // 2
    width = data_ref.shape[2]
    first = pl.multiple_of(core * half, half)
    piece0_ref[...] = data_ref[:, pl.ds(first, half)]
    piece1_ref[...] = data_ref[:, pl.ds(pl.multiple_of(half - first, half), half)]
    weights = jnp.transpose(jnp.concatenate([source_ref[...]] * 4, axis=0))
    weight_re = weights[:, 0:1]
    weight_im = weights[:, 1:2]
    recorded_re = data_ref[0].astype(jnp.float32)
    recorded_im = data_ref[1].astype(jnp.float32)
    scaled_ref[:, :width] = (weight_re * recorded_re - weight_im * recorded_im).astype(jnp.bfloat16)
    scaled_ref[:, width:] = (weight_re * recorded_im + weight_im * recorded_re).astype(jnp.bfloat16)


def begin(data, source_term):
    _, rows, cols = data.shape
    piece = jax.ShapeDtypeStruct((2, rows // 2, cols), jnp.bfloat16)
    return kernel_call(
        begin_kernel,
        (piece, piece, jax.ShapeDtypeStruct((rows, 2 * cols), jnp.bfloat16)),
        [VMEM] * 2,
        [VMEM] * 3,
        (data, source_term),
        6 * rows * cols,
        12 * rows * cols,
    )


def place_kernel(out_ref):
    src = lax.axis_index("src")
    rcv = lax.axis_index("rcv")
    x, y_lo, core = src >> 2, (src >> 1) & 1, src & 1
    z, y_hi = rcv >> 1, rcv & 1
    home = jnp.where(core == y_hi, 1, 0)
    for e in range(8):
        block = (z - e) & 7
        shift_x = (x - (block >> 1)) & 3
        shift_x = jnp.where(core == 0, shift_x, (4 - shift_x) & 3)
        shift_y = (block & 1) ^ y_lo
        out_ref[e] = jnp.where(shift_y == home, 0, 4) + shift_x
    at, away = 2 * home, 2 - 2 * home
    for s, (shift_y, shift_x) in enumerate(((0, 2), (1, at), (0, 0), (0, 1), (0, 3), (1, away), (1, 1), (1, 3))):
        out_ref[8 + s] = jnp.where(home == shift_y, 0, 4) + shift_x
    out_ref[16] = core
    out_ref[17] = y_hi
    out_ref[18] = home


def find_place():
    return kernel_call(place_kernel, jax.ShapeDtypeStruct((19,), jnp.int32), [], SMEM, ())


def pick_kernel(place_ref, at_home_ref, away_ref, out_ref):
    out_ref[...] = jnp.where(place_ref[18] == 1, at_home_ref[...], away_ref[...])


def pick(place, at_home, away):
    return kernel_call(
        pick_kernel,
        jax.ShapeDtypeStruct(away.shape, away.dtype),
        [SMEM, VMEM, VMEM],
        VMEM,
        (place, at_home, away),
        0,
        6 * away.size,
    )


def product_kernel(place_ref, *refs, fill, slots, base, begun, finish, count):
    left, refs = (refs[:8], refs[8:]) if fill else (None, refs)
    held_ref, refs = (None, refs) if fill else (refs[0], refs[1:])
    first_ref, refs = (refs[0], refs[1:]) if begun else (None, refs)
    right, refs = refs[:count], refs[count:]
    if fill:
        held_ref, refs = refs[0], refs[1:]
        for e in range(8):
            held_ref[place_ref[e]] = left[e][...]
    out_ref = refs[0]
    total = refs[1] if finish else out_ref
    home = place_ref[18] == 1
    rows, depth = held_ref.shape[2], held_ref.shape[3]

    def row_block(s):
        return held_ref[s if base is None else place_ref[base + s]].reshape(2 * rows, depth)

    def panel(i):
        if i == 0 and count > len(slots):
            return jnp.where(home, right[0][...], right[count - 1][...])
        return right[i][...]

    for i in range(0, len(slots), 2):
        part = jnp.dot(
            jnp.concatenate([row_block(slots[i]), row_block(slots[i + 1])], axis=1),
            jnp.concatenate([panel(i), panel(i + 1)], axis=0),
            preferred_element_type=jnp.float32,
        )
        if i > 0:
            total[...] += part
        elif begun:
            total[...] = first_ref[...] + part
        else:
            total[...] = part
    if finish:
        cols = out_ref.shape[2]
        out_ref[0] = (total[:rows, :cols] - total[rows:, cols:]).astype(out_ref.dtype)
        out_ref[1] = (total[:rows, cols:] + total[rows:, :cols]).astype(out_ref.dtype)


def product(place, left, right, slots, base=None, first=None, dtype=None):
    fill = isinstance(left, dict)
    lefts = [left[e] for e in range(8)] if fill else [left]
    rows, depth = lefts[0].shape[-2:]
    wide = right[0].shape[1]
    args = (place, *lefts, *([] if first is None else [first]), *right)
    out_shape = [jax.ShapeDtypeStruct((8, 2, rows, depth), jnp.bfloat16)] if fill else []
    scratch = []
    if dtype is None:
        out_shape.append(jax.ShapeDtypeStruct((2 * rows, wide), jnp.float32))
    else:
        out_shape.append(jax.ShapeDtypeStruct((2, rows, wide // 2), dtype))
        scratch = [pltpu.VMEM((2 * rows, wide), jnp.float32)]
    out = kernel_call(
        functools.partial(
            product_kernel,
            fill=fill,
            slots=slots,
            base=base,
            begun=first is not None,
            finish=dtype is not None,
            count=len(right),
        ),
        out_shape,
        [SMEM] + [VMEM] * (len(args) - 1),
        [VMEM] * len(out_shape),
        args,
        4 * len(slots) * rows * depth * wide,
        2 * len(slots) * (2 * rows + wide) * depth,
        scratch,
        12,
    )
    return out if fill else out[0]


def combine_kernel(place_ref, own_ref, other_ref, data_ref, *refs, last):
    if last:
        ahead_ref, mult_ref, all_ref, edge_ref, sums_ref = refs
    else:
        mult_ref, sums_ref, edge_ref = refs
    mult_re = (own_ref[0] + other_ref[0].astype(jnp.float32)).astype(jnp.bfloat16)
    mult_im = (own_ref[1] + other_ref[1].astype(jnp.float32)).astype(jnp.bfloat16)
    mult_ref[0] = mult_re
    mult_ref[1] = mult_im
    rows, cols = mult_re.shape
    lane = lax.broadcasted_iota(jnp.int32, (1, cols), 1) // LINE
    slot = lax.broadcasted_iota(jnp.int32, (1, 128), 1)
    for i in range(rows // LINE):
        span = slice(i * LINE, (i + 1) * LINE)
        m_re = mult_re[span].astype(jnp.float32)
        m_im = mult_im[span].astype(jnp.float32)
        d_re = data_ref[0, span].astype(jnp.float32)
        d_im = data_ref[1, span].astype(jnp.float32)
        terms = (m_re * d_re + m_im * d_im, m_re * d_im - m_im * d_re, m_re * m_re + m_im * m_im)
        along = jnp.concatenate(
            [jnp.sum(term, axis=0, keepdims=True) for term in terms] + [jnp.zeros((1, cols), jnp.float32)], axis=0
        )
        part = jnp.zeros((4, 128), jnp.float32)
        for j in range(cols // LINE):
            block = jnp.sum(jnp.where(lane == j, along, 0.0), axis=1, keepdims=True)
            part = jnp.where(slot == j, block, part)
        sums_ref[pl.ds(4 * i, 4), :] = part
    upper = place_ref[16] == 0
    count = sums_ref.shape[0]
    if last:
        all_ref[:count] = jnp.where(upper, ahead_ref[...], sums_ref[...])
        all_ref[count:] = jnp.where(upper, sums_ref[...], ahead_ref[...])
        edge_ref[...] = jnp.where(upper, sums_ref[count - 4 :], sums_ref[:4])
    else:
        edge_ref[...] = jnp.where(upper, sums_ref[:4], sums_ref[count - 4 :])


def combine(place, own, other, data, ahead=None):
    _, rows, cols = own.shape
    count = 4 * (rows // LINE)
    args = (place, own, other, data)
    mult = jax.ShapeDtypeStruct((2, rows, cols), jnp.bfloat16)
    sums = jax.ShapeDtypeStruct((count, 128), jnp.float32)
    edge = jax.ShapeDtypeStruct((4, 128), jnp.float32)
    if ahead is None:
        out_shape = [mult, sums, edge]
        scratch = []
    else:
        args += (ahead,)
        out_shape = [mult, jax.ShapeDtypeStruct((2 * count, 128), jnp.float32), edge]
        scratch = [pltpu.VMEM((count, 128), jnp.float32)]
    return kernel_call(
        functools.partial(combine_kernel, last=ahead is not None),
        out_shape,
        [SMEM] + [VMEM] * (len(args) - 1),
        [VMEM] * 3,
        args,
        16 * rows * cols,
        24 * rows * cols,
        scratch,
    )


def window_kernel(place_ref, sums_ref, mate_ref, next_ref, out_ref):
    upper = place_ref[16] == 0
    mate, other = mate_ref[...], next_ref[...]
    above = jnp.where(upper, other, mate)
    below = jnp.where(upper, mate, other)
    sums = sums_ref[...]
    count = sums.shape[0]
    out_ref[...] = (
        jnp.concatenate([above, sums[: count - 4]], axis=0) + sums + jnp.concatenate([sums[4:], below], axis=0)
    )


def apply_kernel(place_ref, *refs):
    mults = refs[:2]
    window_ref, across_ref, next_ref, out_ref = refs[2:]
    lower = place_ref[17] == 0
    across, other = across_ref[...], next_ref[...]
    left = jnp.where(lower, other, across)
    right = jnp.where(lower, across, other)
    window = window_ref[...]
    slot = lax.broadcasted_iota(jnp.int32, window.shape, 1)
    cols = out_ref.shape[2]
    last = cols // LINE - 1
    before = jnp.where(slot == 0, pltpu.roll(left, 128 - last, 1), pltpu.roll(window, 1, 1))
    after = jnp.where(slot == last, pltpu.roll(right, last, 1), pltpu.roll(window, 127, 1))
    window = window + before + after
    lane = lax.broadcasted_iota(jnp.int32, (1, cols), 1) // LINE
    core = place_ref[16]
    half = window.shape[0] // 2
    rows = mults[0].shape[1]
    for r, mult_ref in enumerate(mults):
        chunk = jnp.where(core == r, window[:half], window[half:])
        start = jnp.where(core == r, 0, rows)
        for i in range(rows // LINE):
            energy = chunk[4 * i + 2 : 4 * i + 3] + STABILISER
            value = chunk[4 * i : 4 * i + 2] / energy
            spread = jnp.zeros((2, cols), jnp.float32)
            for j in range(last + 1):
                spread = jnp.where(lane == j, value[:, j : j + 1], spread)
            coef_re, coef_im = spread[0:1], spread[1:2]
            span = pl.ds(i * LINE, LINE)
            m_re = mult_ref[0, span].astype(jnp.float32)
            m_im = mult_ref[1, span].astype(jnp.float32)
            into = pl.ds(pl.multiple_of(start + i * LINE, LINE), LINE)
            out_ref[0, into] = (coef_re * m_re - coef_im * m_im).astype(jnp.bfloat16)
            out_ref[1, into] = (coef_re * m_im + coef_im * m_re).astype(jnp.bfloat16)


def on_device(data, source_term):
    place = find_place()
    piece0, piece1, scaled = begin(data, source_term)
    pieces = [piece0, piece1]
    left = [{0: piece} for piece in pieces]
    up = list(pieces)
    down = list(pieces)
    for step in range(1, 5):
        for r in range(2):
            if step < 4 or r == 0:
                up[r] = send(up[r], z_up)
                left[r][step] = up[r]
            if step < 4 or r == 1:
                down[r] = send(down[r], z_down)
                left[r][8 - step] = down[r]

    near = send(scaled, near_y)
    far = send(scaled, far_y)

    hs = send(scaled, swap_core)
    h = pick(place, scaled, hs)
    h1 = send(h, x_apart)
    h2 = send(scaled, home_to_opposite)
    h1s = send(h1, swap_core)
    h2s = send(h2, swap_core)

    f = pick(place, near, far)
    fs = send(f, swap_core)
    f1a = send(f, x_apart)
    f1b = send(fs, x_apart)
    f2 = send(f1a, x_apart)
    f1as = send(f1a, swap_core)
    f1bs = send(f1b, swap_core)
    f2s = send(f2, swap_core)

    na = send(h1, y_beside)
    nb = send(pick(place, h2, h), y_beside)
    nas = send(na, swap_core)
    nbs = send(nb, swap_core)

    held0, part = product(place, left[0], [f, f1a, f1bs, fs, f1b, f1as], (0, 1, 3, 4, 5, 7))
    part = product(place, held0, [f2, f2s], (2, 6), None, part, PARTIAL)
    other0 = send(part, y_across)
    every = [f, f1a, f2, f1bs, fs, f1b, f2s, f1as]
    held1, part = product(place, left[1], every, tuple(range(8)), None, None, PARTIAL)
    other1 = send(part, y_across)
    own0 = product(place, held0, [h2, h, h1, h1s, h2s], (0, 2, 3, 4), 8)
    own1 = product(place, held1, [h2, h, h1, h1s, h2s], (0, 2, 3, 4), 8)
    own0 = product(place, held0, [nb, nbs, na, nas], (1, 5, 6, 7), 8, own0, jnp.float32)
    own1 = product(place, held1, [nb, nbs, na, nas], (1, 5, 6, 7), 8, own1, jnp.float32)

    mult0, sums, edge = combine(place, own0, other0, pieces[0])
    from_next = send(edge, next_src)
    mult1, sums, edge = combine(place, own1, other1, pieces[1], sums)
    from_mate = send(edge, swap_core)
    window = kernel_call(
        window_kernel,
        jax.ShapeDtypeStruct(sums.shape, jnp.float32),
        [SMEM] + [VMEM] * 3,
        VMEM,
        (place, sums, from_mate, from_next),
    )
    from_across = send(window, y_across)
    from_next = send(window, next_rcv)
    return kernel_call(
        apply_kernel,
        jax.ShapeDtypeStruct(data.shape, jnp.bfloat16),
        [SMEM] + [VMEM] * 5,
        VMEM,
        (place, mult0, mult1, window, from_across, from_next),
        12 * data.shape[1] * data.shape[2],
        8 * data.shape[1] * data.shape[2],
    )


def solution(mesh):
    in_specs = (P(None, "src", "rcv"), P(None, "src"))
    out_specs = P(None, "src", "rcv")
    return jax.shard_map(
        on_device, mesh=mesh, in_specs=in_specs, out_specs=out_specs, check_vma=False
    )
```

```python
import functools

import jax
import jax.numpy as jnp
from jax import lax
from jax.experimental import pallas as pl
from jax.experimental.pallas import tpu as pltpu
from jax.sharding import PartitionSpec as P


LINE = 64
STABILISER = 1e-05
AXES = ("src", "rcv")
NX, NY, NZ = 4, 4, 8
PARTIAL = jnp.bfloat16
VMEM = pl.BlockSpec(memory_space=pltpu.VMEM)
SMEM = pl.BlockSpec(memory_space=pltpu.SMEM)


def linear(x, y, z, core):
    return ((x * 2 + y % 2) * 2 + core) * 16 + z * 2 + y // 2


def send(value, target):
    pairs = []
    for x in range(NX):
        for y in range(NY):
            for z in range(NZ):
                for core in range(2):
                    to = target(x, y, z, core)
                    if to is not None:
                        pairs.append((linear(x, y, z, core), linear(to[0] % NX, to[1] % NY, to[2] % NZ, to[3])))
    return lax.ppermute(value, AXES, pairs)


def z_up(x, y, z, core):
    return x, y, z + 1, core


def z_down(x, y, z, core):
    return x, y, z - 1, core


def x_apart(x, y, z, core):
    return x + 1 - 2 * core, y, z, core


def home_to_opposite(x, y, z, core):
    return (x + 2, y, z, core) if core == y // 2 else None


def swap_core(x, y, z, core):
    return x, y, z, 1 - core


def y_across(x, y, z, core):
    return x, y + 2, z, core


def near_y(x, y, z, core):
    if y // 2 == core:
        return None
    return x, 3 - y, z, core


def y_beside(x, y, z, core):
    return x, y ^ 1, z, core


def far_y(x, y, z, core):
    if y // 2 == core:
        return None
    return x, y ^ 2, z, 1 - core


def next_src(x, y, z, core):
    src = (x * 2 + y % 2) * 2 + core + (1 if core else -1)
    if not 0 <= src < 16:
        return None
    return src // 4, y // 2 * 2 + src // 2 % 2, z, src % 2


def beside_rcv(x, y, z, core):
    if core == 0:
        return y_across(x, y, z, core)
    rcv = z * 2 + y // 2 + (1 if y // 2 else -1)
    if not 0 <= rcv < 16:
        return None
    return x, rcv % 2 * 2 + y % 2, rcv // 2, core


def kernel_call(kernel, out_shape, in_specs, out_specs, args, flops=0, moved=0, scratch=(), limit=8):
    return pl.pallas_call(
        kernel,
        out_shape=out_shape,
        in_specs=in_specs,
        out_specs=out_specs,
        scratch_shapes=scratch,
        compiler_params=pltpu.CompilerParams(vmem_limit_bytes=limit << 20),
        cost_estimate=pl.CostEstimate(flops=flops, bytes_accessed=moved, transcendentals=0),
    )(*args)


def begin_kernel(data_ref, piece0_ref, piece1_ref, place_ref, sems):
    src = lax.axis_index("src")
    rcv = lax.axis_index("rcv")
    x, y_lo, core = src >> 2, (src >> 1) & 1, src & 1
    z, y_hi = rcv >> 1, rcv & 1
    half = data_ref.shape[1] // 2
    copies = []
    for r, piece_ref in enumerate((piece0_ref, piece1_ref)):
        start = pl.multiple_of((core if r == 0 else 1 - core) * half, half)
        copies.append(pltpu.make_async_copy(data_ref.at[:, pl.ds(start, half)], piece_ref, sems.at[r]))
        copies[r].start()
    home = jnp.where(core == y_hi, 1, 0)
    for e in range(8):
        block = (z - e) & 7
        shift_x = (x - (block >> 1)) & 3
        shift_x = jnp.where(core == 0, shift_x, (4 - shift_x) & 3)
        shift_y = (block & 1) ^ y_lo
        place_ref[e] = jnp.where(shift_y == home, 0, 4) + shift_x
    at, away = 2 * home, 2 - 2 * home
    for s, (shift_y, shift_x) in enumerate(((0, 2), (1, at), (0, 0), (0, 1), (0, 3), (1, away), (1, 1), (1, 3))):
        place_ref[8 + s] = jnp.where(home == shift_y, 0, 4) + shift_x
    place_ref[16] = core
    place_ref[17] = y_hi
    place_ref[18] = home
    for copy in copies:
        copy.wait()


def begin(data):
    _, rows, cols = data.shape
    piece = jax.ShapeDtypeStruct((2, rows // 2, cols), jnp.bfloat16)
    return kernel_call(
        begin_kernel,
        (piece, piece, jax.ShapeDtypeStruct((19,), jnp.int32)),
        [pl.BlockSpec(memory_space=pl.ANY)],
        [VMEM, VMEM, SMEM],
        (data,),
        0,
        8 * rows * cols,
        [pltpu.SemaphoreType.DMA((2,))],
    )


def scale_kernel(place_ref, source_ref, piece0_ref, piece1_ref, scaled_ref):
    weights = jnp.transpose(jnp.concatenate([source_ref[...]] * 4, axis=0))
    _, half, width = piece0_ref.shape
    for r, piece_ref in enumerate((piece0_ref, piece1_ref)):
        first = place_ref[16] == r
        weight = jnp.where(first, weights[:half], weights[half:])
        rows = pl.ds(pl.multiple_of(jnp.where(first, 0, half), half), half)
        weight_re = weight[:, 0:1]
        weight_im = weight[:, 1:2]
        recorded_re = piece_ref[0].astype(jnp.float32)
        recorded_im = piece_ref[1].astype(jnp.float32)
        scaled_ref[rows, :width] = (weight_re * recorded_re - weight_im * recorded_im).astype(jnp.bfloat16)
        scaled_ref[rows, width:] = (weight_re * recorded_im + weight_im * recorded_re).astype(jnp.bfloat16)


def scale(place, source_term, pieces):
    _, rows, cols = pieces[0].shape
    return kernel_call(
        scale_kernel,
        jax.ShapeDtypeStruct((2 * rows, 2 * cols), jnp.bfloat16),
        [SMEM] + [VMEM] * 3,
        VMEM,
        (place, source_term, *pieces),
        12 * rows * cols,
        16 * rows * cols,
    )


def pick_kernel(place_ref, at_home_ref, away_ref, out_ref):
    out_ref[...] = jnp.where(place_ref[18] == 1, at_home_ref[...], away_ref[...])


def pick(place, at_home, away):
    return kernel_call(
        pick_kernel,
        jax.ShapeDtypeStruct(away.shape, away.dtype),
        [SMEM, VMEM, VMEM],
        VMEM,
        (place, at_home, away),
        0,
        6 * away.size,
    )


def product_kernel(place_ref, *refs, fill, slots, base, begun, finish, count):
    left, refs = (refs[:8], refs[8:]) if fill else (None, refs)
    held_ref, refs = (None, refs) if fill else (refs[0], refs[1:])
    first_ref, refs = (refs[0], refs[1:]) if begun else (None, refs)
    right, refs = refs[:count], refs[count:]
    if fill:
        held_ref, refs = refs[0], refs[1:]
        for e in range(8):
            held_ref[place_ref[e]] = left[e][...]
    out_ref = refs[0]
    total = refs[1] if finish else out_ref
    home = place_ref[18] == 1
    rows, depth = held_ref.shape[2], held_ref.shape[3]

    def row_block(s):
        return held_ref[s if base is None else place_ref[base + s]].reshape(2 * rows, depth)

    def panel(i):
        if i == 0 and count > len(slots):
            return jnp.where(home, right[0][...], right[count - 1][...])
        return right[i][...]

    for i in range(0, len(slots), 2):
        part = jnp.dot(
            jnp.concatenate([row_block(slots[i]), row_block(slots[i + 1])], axis=1),
            jnp.concatenate([panel(i), panel(i + 1)], axis=0),
            preferred_element_type=jnp.float32,
        )
        if i > 0:
            total[...] += part
        elif begun:
            total[...] = first_ref[...] + part
        else:
            total[...] = part
    if finish:
        cols = out_ref.shape[2]
        out_ref[0] = (total[:rows, :cols] - total[rows:, cols:]).astype(out_ref.dtype)
        out_ref[1] = (total[:rows, cols:] + total[rows:, :cols]).astype(out_ref.dtype)


def product(place, left, right, slots, base=None, first=None, dtype=None):
    fill = isinstance(left, dict)
    lefts = [left[e] for e in range(8)] if fill else [left]
    rows, depth = lefts[0].shape[-2:]
    wide = right[0].shape[1]
    args = (place, *lefts, *([] if first is None else [first]), *right)
    out_shape = [jax.ShapeDtypeStruct((8, 2, rows, depth), jnp.bfloat16)] if fill else []
    scratch = []
    if dtype is None:
        out_shape.append(jax.ShapeDtypeStruct((2 * rows, wide), jnp.float32))
    else:
        out_shape.append(jax.ShapeDtypeStruct((2, rows, wide // 2), dtype))
        scratch = [pltpu.VMEM((2 * rows, wide), jnp.float32)]
    out = kernel_call(
        functools.partial(
            product_kernel,
            fill=fill,
            slots=slots,
            base=base,
            begun=first is not None,
            finish=dtype is not None,
            count=len(right),
        ),
        out_shape,
        [SMEM] + [VMEM] * (len(args) - 1),
        [VMEM] * len(out_shape),
        args,
        4 * len(slots) * rows * depth * wide,
        2 * len(slots) * (2 * rows + wide) * depth,
        scratch,
        12,
    )
    return out if fill else out[0]


def combine_kernel(place_ref, own_ref, other_ref, data_ref, *refs, last):
    if last:
        ahead_ref, next_ref, mult_ref, pack_ref, sums_ref = refs
    else:
        mult_ref, sums_ref, edge_ref = refs
    mult_re = (own_ref[0] + other_ref[0].astype(jnp.float32)).astype(jnp.bfloat16)
    mult_im = (own_ref[1] + other_ref[1].astype(jnp.float32)).astype(jnp.bfloat16)
    mult_ref[0] = mult_re
    mult_ref[1] = mult_im
    rows, cols = mult_re.shape
    lane = lax.broadcasted_iota(jnp.int32, (1, cols), 1) // LINE
    slot = lax.broadcasted_iota(jnp.int32, (1, 128), 1)
    for i in range(rows // LINE):
        span = slice(i * LINE, (i + 1) * LINE)
        m_re = mult_re[span].astype(jnp.float32)
        m_im = mult_im[span].astype(jnp.float32)
        d_re = data_ref[0, span].astype(jnp.float32)
        d_im = data_ref[1, span].astype(jnp.float32)
        terms = (m_re * d_re + m_im * d_im, m_re * d_im - m_im * d_re, m_re * m_re + m_im * m_im)
        along = jnp.concatenate(
            [jnp.sum(term, axis=0, keepdims=True) for term in terms] + [jnp.zeros((1, cols), jnp.float32)], axis=0
        )
        part = jnp.zeros((4, 128), jnp.float32)
        for j in range(cols // LINE):
            block = jnp.sum(jnp.where(lane == j, along, 0.0), axis=1, keepdims=True)
            part = jnp.where(slot == j, block, part)
        sums_ref[pl.ds(4 * i, 4), :] = part
    upper = place_ref[16] == 0
    count = sums_ref.shape[0]
    if last:
        pack_ref[:count] = jnp.where(upper, ahead_ref[...], sums_ref[...])
        pack_ref[count : 2 * count] = jnp.where(upper, sums_ref[...], ahead_ref[...])
        pack_ref[2 * count : 2 * count + 4] = next_ref[...]
        pack_ref[2 * count + 4 :] = jnp.zeros_like(next_ref)
    else:
        edge_ref[...] = jnp.where(upper, sums_ref[:4], sums_ref[count - 4 :])


def combine(place, own, other, data, ahead=None, from_next=None):
    _, rows, cols = own.shape
    count = 4 * (rows // LINE)
    args = (place, own, other, data)
    mult = jax.ShapeDtypeStruct((2, rows, cols), jnp.bfloat16)
    sums = jax.ShapeDtypeStruct((count, 128), jnp.float32)
    if ahead is None:
        out_shape = [mult, sums, jax.ShapeDtypeStruct((4, 128), jnp.float32)]
        scratch = []
    else:
        args += (ahead, from_next)
        out_shape = [mult, jax.ShapeDtypeStruct((2 * count + 8, 128), jnp.float32)]
        scratch = [pltpu.VMEM((count, 128), jnp.float32)]
    return kernel_call(
        functools.partial(combine_kernel, last=ahead is not None),
        out_shape,
        [SMEM] + [VMEM] * (len(args) - 1),
        [VMEM] * len(out_shape),
        args,
        16 * rows * cols,
        24 * rows * cols,
        scratch,
    )


def window_kernel(place_ref, mine_ref, mate_ref, out_ref):
    upper = place_ref[16] == 0
    mine, mate = mine_ref[...], mate_ref[...]
    first = jnp.where(upper, mine, mate)
    second = jnp.where(upper, mate, mine)
    count = first.shape[0] - 8
    tall = jnp.concatenate(
        [first[count : count + 4], first[:count], second[:count], second[count : count + 4]], axis=0
    )
    out_ref[...] = tall[: 2 * count] + tall[4 : 2 * count + 4] + tall[8:]


def apply_kernel(place_ref, *refs):
    mults = refs[:2]
    window_ref, heard_ref, mate_ref, out_ref = refs[2:]
    lower = place_ref[17] == 0
    upper = place_ref[16] == 0
    count = window_ref.shape[0] // 2
    heard, mate = heard_ref[...], mate_ref[...]
    across = jnp.where(upper, heard[:count], mate[count:])
    other = jnp.where(upper, mate[:count], heard[count:])
    left = jnp.where(lower, other, across)
    right = jnp.where(lower, across, other)
    window = jnp.where(upper, window_ref[:count], window_ref[count:])
    slot = lax.broadcasted_iota(jnp.int32, window.shape, 1)
    cols = out_ref.shape[2]
    last = cols // LINE - 1
    before = jnp.where(slot == 0, pltpu.roll(left, 128 - last, 1), pltpu.roll(window, 1, 1))
    after = jnp.where(slot == last, pltpu.roll(right, last, 1), pltpu.roll(window, 127, 1))
    window = window + before + after
    lane = lax.broadcasted_iota(jnp.int32, (1, cols), 1) // LINE
    core = place_ref[16]
    half = window.shape[0] // 2
    rows = mults[0].shape[1]
    for r, mult_ref in enumerate(mults):
        chunk = jnp.where(core == r, window[:half], window[half:])
        start = jnp.where(core == r, 0, rows)
        for i in range(rows // LINE):
            energy = chunk[4 * i + 2 : 4 * i + 3] + STABILISER
            value = chunk[4 * i : 4 * i + 2] / energy
            spread = jnp.zeros((2, cols), jnp.float32)
            for j in range(last + 1):
                spread = jnp.where(lane == j, value[:, j : j + 1], spread)
            coef_re, coef_im = spread[0:1], spread[1:2]
            span = pl.ds(i * LINE, LINE)
            m_re = mult_ref[0, span].astype(jnp.float32)
            m_im = mult_ref[1, span].astype(jnp.float32)
            into = pl.ds(pl.multiple_of(start + i * LINE, LINE), LINE)
            out_ref[0, into] = (coef_re * m_re - coef_im * m_im).astype(jnp.bfloat16)
            out_ref[1, into] = (coef_re * m_im + coef_im * m_re).astype(jnp.bfloat16)


def on_device(data, source_term):
    piece0, piece1, place = begin(data)
    pieces = [piece0, piece1]
    scaled = scale(place, source_term, pieces)
    left = [{0: piece} for piece in pieces]
    up = list(pieces)
    down = list(pieces)
    for step in range(1, 5):
        for r in range(2):
            if step < 4 or r == 0:
                up[r] = send(up[r], z_up)
                left[r][step] = up[r]
            if step < 4 or r == 1:
                down[r] = send(down[r], z_down)
                left[r][8 - step] = down[r]

    near = send(scaled, near_y)
    far = send(scaled, far_y)

    hs = send(scaled, swap_core)
    h = pick(place, scaled, hs)
    h1 = send(h, x_apart)
    h2 = send(scaled, home_to_opposite)
    h1s = send(h1, swap_core)
    h2s = send(h2, swap_core)

    f = pick(place, near, far)
    fs = send(f, swap_core)
    f1a = send(f, x_apart)
    f1b = send(fs, x_apart)
    f2 = send(f1a, x_apart)
    f1as = send(f1a, swap_core)
    f1bs = send(f1b, swap_core)
    f2s = send(f2, swap_core)

    na = send(h1, y_beside)
    nb = send(pick(place, h2, h), y_beside)
    nas = send(na, swap_core)
    nbs = send(nb, swap_core)

    held0, part = product(place, left[0], [f, f1a, f1bs, fs, f1b, f1as], (0, 1, 3, 4, 5, 7))
    part = product(place, held0, [f2, f2s], (2, 6), None, part, PARTIAL)
    other0 = send(part, y_across)
    every = [f, f1a, f2, f1bs, fs, f1b, f2s, f1as]
    held1, part = product(place, left[1], every, tuple(range(8)), None, None, PARTIAL)
    other1 = send(part, y_across)
    own0 = product(place, held0, [h2, h, h1, h1s, h2s], (0, 2, 3, 4), 8)
    own0 = product(place, held0, [nb, nbs, na, nas], (1, 5, 6, 7), 8, own0, jnp.float32)
    every = [h2, nb, h, h1, h1s, nbs, na, nas, h2s]
    own1 = product(place, held1, every, tuple(range(8)), 8, None, jnp.float32)

    mult0, sums, edge = combine(place, own0, other0, pieces[0])
    from_next = send(edge, next_src)
    mult1, pack = combine(place, own1, other1, pieces[1], sums, from_next)
    from_mate = send(pack, swap_core)
    window = kernel_call(
        window_kernel,
        jax.ShapeDtypeStruct((2 * (pack.shape[0] - 8), 128), jnp.float32),
        [SMEM] + [VMEM] * 2,
        VMEM,
        (place, pack, from_mate),
    )
    heard = send(window, beside_rcv)
    from_mate = send(heard, swap_core)
    return kernel_call(
        apply_kernel,
        jax.ShapeDtypeStruct(data.shape, jnp.bfloat16),
        [SMEM] + [VMEM] * 5,
        VMEM,
        (place, mult0, mult1, window, heard, from_mate),
        12 * data.shape[1] * data.shape[2],
        8 * data.shape[1] * data.shape[2],
    )


def solution(mesh):
    in_specs = (P(None, "src", "rcv"), P(None, "src"))
    out_specs = P(None, "src", "rcv")
    return jax.shard_map(
        on_device, mesh=mesh, in_specs=in_specs, out_specs=out_specs, check_vma=False
    )
```

```python
import functools

import jax
import jax.numpy as jnp
from jax import lax
from jax.experimental import pallas as pl
from jax.experimental.pallas import tpu as pltpu
from jax.sharding import PartitionSpec as P


LINE = 64
STABILISER = 1e-05
AXES = ("src", "rcv")
NX, NY, NZ = 4, 4, 8
PARTIAL = jnp.bfloat16
VMEM = pl.BlockSpec(memory_space=pltpu.VMEM)
SMEM = pl.BlockSpec(memory_space=pltpu.SMEM)


def linear(x, y, z, core):
    return ((x * 2 + y % 2) * 2 + core) * 16 + z * 2 + y // 2


def send(value, target):
    pairs = []
    for x in range(NX):
        for y in range(NY):
            for z in range(NZ):
                for core in range(2):
                    to = target(x, y, z, core)
                    if to is not None:
                        pairs.append((linear(x, y, z, core), linear(to[0] % NX, to[1] % NY, to[2] % NZ, to[3])))
    return lax.ppermute(value, AXES, pairs)


def z_up(x, y, z, core):
    return x, y, z + 1, core


def z_down(x, y, z, core):
    return x, y, z - 1, core


def x_apart(x, y, z, core):
    return x + 1 - 2 * core, y, z, core


def home_to_opposite(x, y, z, core):
    return (x + 2, y, z, core) if core == y // 2 else None


def swap_core(x, y, z, core):
    return x, y, z, 1 - core


def y_across(x, y, z, core):
    return x, y + 2, z, core


def near_y(x, y, z, core):
    if y // 2 == core:
        return None
    return x, 3 - y, z, core


def y_beside(x, y, z, core):
    return x, y ^ 1, z, core


def far_y(x, y, z, core):
    if y // 2 == core:
        return None
    return x, y ^ 2, z, 1 - core


def next_src(x, y, z, core):
    src = (x * 2 + y % 2) * 2 + core + (1 if core else -1)
    if not 0 <= src < 16:
        return None
    return src // 4, y // 2 * 2 + src // 2 % 2, z, src % 2


def beside_rcv(x, y, z, core):
    if core == 0:
        return y_across(x, y, z, core)
    rcv = z * 2 + y // 2 + (1 if y // 2 else -1)
    if not 0 <= rcv < 16:
        return None
    return x, rcv % 2 * 2 + y % 2, rcv // 2, core


def kernel_call(kernel, out_shape, in_specs, out_specs, args, flops=0, moved=0, scratch=(), limit=8):
    return pl.pallas_call(
        kernel,
        out_shape=out_shape,
        in_specs=in_specs,
        out_specs=out_specs,
        scratch_shapes=scratch,
        compiler_params=pltpu.CompilerParams(vmem_limit_bytes=limit << 20),
        cost_estimate=pl.CostEstimate(flops=flops, bytes_accessed=moved, transcendentals=0),
    )(*args)


def begin_kernel(data_ref, piece0_ref, piece1_ref, place_ref, sems):
    src = lax.axis_index("src")
    rcv = lax.axis_index("rcv")
    x, y_lo, core = src >> 2, (src >> 1) & 1, src & 1
    z, y_hi = rcv >> 1, rcv & 1
    half = data_ref.shape[1] // 2
    copies = []
    for r, piece_ref in enumerate((piece0_ref, piece1_ref)):
        start = pl.multiple_of((core if r == 0 else 1 - core) * half, half)
        copies.append(pltpu.make_async_copy(data_ref.at[:, pl.ds(start, half)], piece_ref, sems.at[r]))
        copies[r].start()
    home = jnp.where(core == y_hi, 1, 0)
    for e in range(8):
        block = (z - e) & 7
        shift_x = (x - (block >> 1)) & 3
        shift_x = jnp.where(core == 0, shift_x, (4 - shift_x) & 3)
        shift_y = (block & 1) ^ y_lo
        place_ref[e] = jnp.where(shift_y == home, 0, 4) + shift_x
    at, away = 2 * home, 2 - 2 * home
    for s, (shift_y, shift_x) in enumerate(((0, 2), (1, at), (0, 0), (0, 1), (0, 3), (1, away), (1, 1), (1, 3))):
        place_ref[8 + s] = jnp.where(home == shift_y, 0, 4) + shift_x
    place_ref[16] = core
    place_ref[17] = y_hi
    place_ref[18] = home
    for copy in copies:
        copy.wait()


def begin(data):
    _, rows, cols = data.shape
    piece = jax.ShapeDtypeStruct((2, rows // 2, cols), jnp.bfloat16)
    return kernel_call(
        begin_kernel,
        (piece, piece, jax.ShapeDtypeStruct((19,), jnp.int32)),
        [pl.BlockSpec(memory_space=pl.ANY)],
        [VMEM, VMEM, SMEM],
        (data,),
        0,
        8 * rows * cols,
        [pltpu.SemaphoreType.DMA((2,))],
    )


def scale_kernel(place_ref, source_ref, piece0_ref, piece1_ref, scaled_ref):
    weights = jnp.transpose(jnp.concatenate([source_ref[...]] * 4, axis=0))
    _, half, width = piece0_ref.shape
    for r, piece_ref in enumerate((piece0_ref, piece1_ref)):
        first = place_ref[16] == r
        weight = jnp.where(first, weights[:half], weights[half:])
        rows = pl.ds(pl.multiple_of(jnp.where(first, 0, half), half), half)
        weight_re = weight[:, 0:1]
        weight_im = weight[:, 1:2]
        recorded_re = piece_ref[0].astype(jnp.float32)
        recorded_im = piece_ref[1].astype(jnp.float32)
        scaled_ref[rows, :width] = (weight_re * recorded_re - weight_im * recorded_im).astype(jnp.bfloat16)
        scaled_ref[rows, width:] = (weight_re * recorded_im + weight_im * recorded_re).astype(jnp.bfloat16)


def scale(place, source_term, pieces):
    _, rows, cols = pieces[0].shape
    return kernel_call(
        scale_kernel,
        jax.ShapeDtypeStruct((2 * rows, 2 * cols), jnp.bfloat16),
        [SMEM] + [VMEM] * 3,
        VMEM,
        (place, source_term, *pieces),
        12 * rows * cols,
        16 * rows * cols,
    )


def pick_kernel(place_ref, at_home_ref, away_ref, out_ref):
    out_ref[...] = jnp.where(place_ref[18] == 1, at_home_ref[...], away_ref[...])


def pick(place, at_home, away):
    return kernel_call(
        pick_kernel,
        jax.ShapeDtypeStruct(away.shape, away.dtype),
        [SMEM, VMEM, VMEM],
        VMEM,
        (place, at_home, away),
        0,
        6 * away.size,
    )


def product_kernel(place_ref, *refs, fill, slots, base, begun, finish, count):
    left, refs = (refs[:8], refs[8:]) if fill else (None, refs)
    held_ref, refs = (None, refs) if fill else (refs[0], refs[1:])
    first_ref, refs = (refs[0], refs[1:]) if begun else (None, refs)
    right, refs = refs[:count], refs[count:]
    if fill:
        held_ref, refs = refs[0], refs[1:]
        for e in range(8):
            held_ref[place_ref[e]] = left[e][...]
    out_ref = refs[0]
    total = refs[1] if finish else out_ref
    home = place_ref[18] == 1
    rows, depth = held_ref.shape[2], held_ref.shape[3]

    def row_block(s):
        return held_ref[s if base is None else place_ref[base + s]].reshape(2 * rows, depth)

    def panel(i):
        if i == 0 and count > len(slots):
            return jnp.where(home, right[0][...], right[count - 1][...])
        return right[i][...]

    for i in range(0, len(slots), 2):
        part = jnp.dot(
            jnp.concatenate([row_block(slots[i]), row_block(slots[i + 1])], axis=1),
            jnp.concatenate([panel(i), panel(i + 1)], axis=0),
            preferred_element_type=jnp.float32,
        )
        if i > 0:
            total[...] += part
        elif begun:
            total[...] = first_ref[...] + part
        else:
            total[...] = part
    if finish:
        cols = out_ref.shape[2]
        out_ref[0] = (total[:rows, :cols] - total[rows:, cols:]).astype(out_ref.dtype)
        out_ref[1] = (total[:rows, cols:] + total[rows:, :cols]).astype(out_ref.dtype)


def product(place, left, right, slots, base=None, first=None, dtype=None):
    fill = isinstance(left, dict)
    lefts = [left[e] for e in range(8)] if fill else [left]
    rows, depth = lefts[0].shape[-2:]
    wide = right[0].shape[1]
    args = (place, *lefts, *([] if first is None else [first]), *right)
    out_shape = [jax.ShapeDtypeStruct((8, 2, rows, depth), jnp.bfloat16)] if fill else []
    scratch = []
    if dtype is None:
        out_shape.append(jax.ShapeDtypeStruct((2 * rows, wide), jnp.float32))
    else:
        out_shape.append(jax.ShapeDtypeStruct((2, rows, wide // 2), dtype))
        scratch = [pltpu.VMEM((2 * rows, wide), jnp.float32)]
    out = kernel_call(
        functools.partial(
            product_kernel,
            fill=fill,
            slots=slots,
            base=base,
            begun=first is not None,
            finish=dtype is not None,
            count=len(right),
        ),
        out_shape,
        [SMEM] + [VMEM] * (len(args) - 1),
        [VMEM] * len(out_shape),
        args,
        4 * len(slots) * rows * depth * wide,
        2 * len(slots) * (2 * rows + wide) * depth,
        scratch,
        12,
    )
    return out if fill else out[0]


def combine_kernel(place_ref, own_ref, other_ref, data_ref, *refs, last):
    if last:
        ahead_ref, next_ref, mult_ref, pack_ref, sums_ref = refs
    else:
        mult_ref, sums_ref, edge_ref = refs
    mult_re = (own_ref[0] + other_ref[0].astype(jnp.float32)).astype(jnp.bfloat16)
    mult_im = (own_ref[1] + other_ref[1].astype(jnp.float32)).astype(jnp.bfloat16)
    mult_ref[0] = mult_re
    mult_ref[1] = mult_im
    rows, cols = mult_re.shape
    lane = lax.broadcasted_iota(jnp.int32, (1, cols), 1) // LINE
    slot = lax.broadcasted_iota(jnp.int32, (1, 128), 1)
    for i in range(rows // LINE):
        span = slice(i * LINE, (i + 1) * LINE)
        m_re = mult_re[span].astype(jnp.float32)
        m_im = mult_im[span].astype(jnp.float32)
        d_re = data_ref[0, span].astype(jnp.float32)
        d_im = data_ref[1, span].astype(jnp.float32)
        terms = (m_re * d_re + m_im * d_im, m_re * d_im - m_im * d_re, m_re * m_re + m_im * m_im)
        along = jnp.concatenate(
            [jnp.sum(term, axis=0, keepdims=True) for term in terms] + [jnp.zeros((1, cols), jnp.float32)], axis=0
        )
        part = jnp.zeros((4, 128), jnp.float32)
        for j in range(cols // LINE):
            block = jnp.sum(jnp.where(lane == j, along, 0.0), axis=1, keepdims=True)
            part = jnp.where(slot == j, block, part)
        sums_ref[pl.ds(4 * i, 4), :] = part
    upper = place_ref[16] == 0
    count = sums_ref.shape[0]
    if last:
        pack_ref[:count] = jnp.where(upper, ahead_ref[...], sums_ref[...])
        pack_ref[count : 2 * count] = jnp.where(upper, sums_ref[...], ahead_ref[...])
        pack_ref[2 * count : 2 * count + 4] = next_ref[...]
        pack_ref[2 * count + 4 :] = jnp.zeros_like(next_ref)
    else:
        edge_ref[...] = jnp.where(upper, sums_ref[:4], sums_ref[count - 4 :])


def combine(place, own, other, data, ahead=None, from_next=None):
    _, rows, cols = own.shape
    count = 4 * (rows // LINE)
    args = (place, own, other, data)
    mult = jax.ShapeDtypeStruct((2, rows, cols), jnp.bfloat16)
    sums = jax.ShapeDtypeStruct((count, 128), jnp.float32)
    if ahead is None:
        out_shape = [mult, sums, jax.ShapeDtypeStruct((4, 128), jnp.float32)]
        scratch = []
    else:
        args += (ahead, from_next)
        out_shape = [mult, jax.ShapeDtypeStruct((2 * count + 8, 128), jnp.float32)]
        scratch = [pltpu.VMEM((count, 128), jnp.float32)]
    return kernel_call(
        functools.partial(combine_kernel, last=ahead is not None),
        out_shape,
        [SMEM] + [VMEM] * (len(args) - 1),
        [VMEM] * len(out_shape),
        args,
        16 * rows * cols,
        24 * rows * cols,
        scratch,
    )


def window_kernel(place_ref, mine_ref, mate_ref, out_ref):
    upper = place_ref[16] == 0
    mine, mate = mine_ref[...], mate_ref[...]
    first = jnp.where(upper, mine, mate)
    second = jnp.where(upper, mate, mine)
    count = first.shape[0] - 8
    tall = jnp.concatenate(
        [first[count : count + 4], first[:count], second[:count], second[count : count + 4]], axis=0
    )
    out_ref[...] = tall[: 2 * count] + tall[4 : 2 * count + 4] + tall[8:]


def apply_kernel(place_ref, *refs):
    mults = refs[:2]
    window_ref, heard_ref, mate_ref, out_ref, filtered, sems = refs[2:]
    copies = []
    lower = place_ref[17] == 0
    upper = place_ref[16] == 0
    count = window_ref.shape[0] // 2
    heard, mate = heard_ref[...], mate_ref[...]
    across = jnp.where(upper, heard[:count], mate[count:])
    other = jnp.where(upper, mate[:count], heard[count:])
    left = jnp.where(lower, other, across)
    right = jnp.where(lower, across, other)
    window = jnp.where(upper, window_ref[:count], window_ref[count:])
    slot = lax.broadcasted_iota(jnp.int32, window.shape, 1)
    cols = out_ref.shape[2]
    last = cols // LINE - 1
    before = jnp.where(slot == 0, pltpu.roll(left, 128 - last, 1), pltpu.roll(window, 1, 1))
    after = jnp.where(slot == last, pltpu.roll(right, last, 1), pltpu.roll(window, 127, 1))
    window = window + before + after
    lane = lax.broadcasted_iota(jnp.int32, (1, cols), 1) // LINE
    core = place_ref[16]
    half = window.shape[0] // 2
    rows = mults[0].shape[1]
    for r, mult_ref in enumerate(mults):
        chunk = jnp.where(core == r, window[:half], window[half:])
        start = jnp.where(core == r, 0, rows)
        for i in range(rows // LINE):
            energy = chunk[4 * i + 2 : 4 * i + 3] + STABILISER
            value = chunk[4 * i : 4 * i + 2] / energy
            spread = jnp.zeros((2, cols), jnp.float32)
            for j in range(last + 1):
                spread = jnp.where(lane == j, value[:, j : j + 1], spread)
            coef_re, coef_im = spread[0:1], spread[1:2]
            span = pl.ds(i * LINE, LINE)
            m_re = mult_ref[0, span].astype(jnp.float32)
            m_im = mult_ref[1, span].astype(jnp.float32)
            filtered[r, 0, span] = (coef_re * m_re - coef_im * m_im).astype(jnp.bfloat16)
            filtered[r, 1, span] = (coef_re * m_im + coef_im * m_re).astype(jnp.bfloat16)
        into = out_ref.at[:, pl.ds(pl.multiple_of(start, rows), rows)]
        copies.append(pltpu.make_async_copy(filtered.at[r], into, sems.at[r]))
        copies[r].start()
    for copy in copies:
        copy.wait()


def on_device(data, source_term):
    piece0, piece1, place = begin(data)
    pieces = [piece0, piece1]
    scaled = scale(place, source_term, pieces)
    left = [{0: piece} for piece in pieces]
    up = list(pieces)
    down = list(pieces)
    for step in range(1, 5):
        for r in range(2):
            if step < 4 or r == 0:
                up[r] = send(up[r], z_up)
                left[r][step] = up[r]
            if step < 4 or r == 1:
                down[r] = send(down[r], z_down)
                left[r][8 - step] = down[r]

    near = send(scaled, near_y)
    far = send(scaled, far_y)

    hs = send(scaled, swap_core)
    h = pick(place, scaled, hs)
    h1 = send(h, x_apart)
    h2 = send(scaled, home_to_opposite)
    h1s = send(h1, swap_core)
    h2s = send(h2, swap_core)

    f = pick(place, near, far)
    fs = send(f, swap_core)
    f1a = send(f, x_apart)
    f1b = send(fs, x_apart)
    f2 = send(f1a, x_apart)
    f1as = send(f1a, swap_core)
    f1bs = send(f1b, swap_core)
    f2s = send(f2, swap_core)

    na = send(h1, y_beside)
    nb = send(pick(place, h2, h), y_beside)
    nas = send(na, swap_core)
    nbs = send(nb, swap_core)

    held0, part = product(place, left[0], [f, f1a, f1bs, fs, f1b, f1as], (0, 1, 3, 4, 5, 7))
    part = product(place, held0, [f2, f2s], (2, 6), None, part, PARTIAL)
    other0 = send(part, y_across)
    every = [f, f1a, f2, f1bs, fs, f1b, f2s, f1as]
    held1, part = product(place, left[1], every, tuple(range(8)), None, None, PARTIAL)
    other1 = send(part, y_across)
    every = [h2, nb, h, h1, h1s, nbs, na, nas, h2s]
    own0 = product(place, held0, every, tuple(range(8)), 8, None, jnp.float32)
    own1 = product(place, held1, every, tuple(range(8)), 8, None, jnp.float32)

    mult0, sums, edge = combine(place, own0, other0, pieces[0])
    from_next = send(edge, next_src)
    mult1, pack = combine(place, own1, other1, pieces[1], sums, from_next)
    from_mate = send(pack, swap_core)
    window = kernel_call(
        window_kernel,
        jax.ShapeDtypeStruct((2 * (pack.shape[0] - 8), 128), jnp.float32),
        [SMEM] + [VMEM] * 2,
        VMEM,
        (place, pack, from_mate),
    )
    heard = send(window, beside_rcv)
    from_mate = send(heard, swap_core)
    return kernel_call(
        apply_kernel,
        jax.ShapeDtypeStruct(data.shape, jnp.bfloat16),
        [SMEM] + [VMEM] * 5,
        pl.BlockSpec(memory_space=pl.ANY),
        (place, mult0, mult1, window, heard, from_mate),
        12 * data.shape[1] * data.shape[2],
        8 * data.shape[1] * data.shape[2],
        [pltpu.VMEM((2, *mult0.shape), jnp.bfloat16), pltpu.SemaphoreType.DMA((2,))],
    )


def solution(mesh):
    in_specs = (P(None, "src", "rcv"), P(None, "src"))
    out_specs = P(None, "src", "rcv")
    return jax.shard_map(
        on_device, mesh=mesh, in_specs=in_specs, out_specs=out_specs, check_vma=False
    )
```

```python
import functools

import jax
import jax.numpy as jnp
from jax import lax
from jax.experimental import pallas as pl
from jax.experimental.pallas import tpu as pltpu
from jax.sharding import PartitionSpec as P


LINE = 64
STABILISER = 1e-05
AXES = ("src", "rcv")
NX, NY, NZ = 4, 4, 8
PARTIAL = jnp.bfloat16
VMEM = pl.BlockSpec(memory_space=pltpu.VMEM)
SMEM = pl.BlockSpec(memory_space=pltpu.SMEM)


def linear(x, y, z, core):
    return ((x * 2 + y % 2) * 2 + core) * 16 + z * 2 + y // 2


def send(value, target):
    pairs = []
    for x in range(NX):
        for y in range(NY):
            for z in range(NZ):
                for core in range(2):
                    to = target(x, y, z, core)
                    if to is not None:
                        pairs.append((linear(x, y, z, core), linear(to[0] % NX, to[1] % NY, to[2] % NZ, to[3])))
    return lax.ppermute(value, AXES, pairs)


def z_up(x, y, z, core):
    return x, y, z + 1, core


def z_down(x, y, z, core):
    return x, y, z - 1, core


def x_apart(x, y, z, core):
    return x + 1 - 2 * core, y, z, core


def home_to_opposite(x, y, z, core):
    return (x + 2, y, z, core) if core == y // 2 else None


def swap_core(x, y, z, core):
    return x, y, z, 1 - core


def y_across(x, y, z, core):
    return x, y + 2, z, core


def near_y(x, y, z, core):
    if y // 2 == core:
        return None
    return x, 3 - y, z, core


def y_beside(x, y, z, core):
    return x, y ^ 1, z, core


def far_y(x, y, z, core):
    if y // 2 == core:
        return None
    return x, y ^ 2, z, 1 - core


def next_src(x, y, z, core):
    src = (x * 2 + y % 2) * 2 + core + (1 if core else -1)
    if not 0 <= src < 16:
        return None
    return src // 4, y // 2 * 2 + src // 2 % 2, z, src % 2


def beside_rcv(x, y, z, core):
    if core == 0:
        return y_across(x, y, z, core)
    rcv = z * 2 + y // 2 + (1 if y // 2 else -1)
    if not 0 <= rcv < 16:
        return None
    return x, rcv % 2 * 2 + y % 2, rcv // 2, core


def kernel_call(kernel, out_shape, in_specs, out_specs, args, flops=0, moved=0, scratch=(), limit=8):
    return pl.pallas_call(
        kernel,
        out_shape=out_shape,
        in_specs=in_specs,
        out_specs=out_specs,
        scratch_shapes=scratch,
        compiler_params=pltpu.CompilerParams(vmem_limit_bytes=limit << 20),
        cost_estimate=pl.CostEstimate(flops=flops, bytes_accessed=moved, transcendentals=0),
    )(*args)


def begin_kernel(data_ref, piece0_ref, piece1_ref, place_ref):
    src = lax.axis_index("src")
    rcv = lax.axis_index("rcv")
    x, y_lo, core = src >> 2, (src >> 1) & 1, src & 1
    z, y_hi = rcv >> 1, rcv & 1
    half = data_ref.shape[1] // 2
    for r, piece_ref in enumerate((piece0_ref, piece1_ref)):
        start = pl.multiple_of((core if r == 0 else 1 - core) * half, half)
        piece_ref[...] = data_ref[:, pl.ds(start, half)]
    home = jnp.where(core == y_hi, 1, 0)
    for e in range(8):
        block = (z - e) & 7
        shift_x = (x - (block >> 1)) & 3
        shift_x = jnp.where(core == 0, shift_x, (4 - shift_x) & 3)
        shift_y = (block & 1) ^ y_lo
        place_ref[e] = jnp.where(shift_y == home, 0, 4) + shift_x
    at, away = 2 * home, 2 - 2 * home
    for s, (shift_y, shift_x) in enumerate(((0, 2), (1, at), (0, 0), (0, 1), (0, 3), (1, away), (1, 1), (1, 3))):
        place_ref[8 + s] = jnp.where(home == shift_y, 0, 4) + shift_x
    place_ref[16] = core
    place_ref[17] = y_hi
    place_ref[18] = home


def begin(data):
    _, rows, cols = data.shape
    piece = jax.ShapeDtypeStruct((2, rows // 2, cols), jnp.bfloat16)
    return kernel_call(
        begin_kernel,
        (piece, piece, jax.ShapeDtypeStruct((19,), jnp.int32)),
        [VMEM],
        [VMEM, VMEM, SMEM],
        (data,),
        0,
        8 * rows * cols,
    )


def scale_kernel(place_ref, source_ref, piece0_ref, piece1_ref, scaled_ref):
    weights = jnp.transpose(jnp.concatenate([source_ref[...]] * 4, axis=0))
    _, half, width = piece0_ref.shape
    for r, piece_ref in enumerate((piece0_ref, piece1_ref)):
        first = place_ref[16] == r
        weight = jnp.where(first, weights[:half], weights[half:])
        rows = pl.ds(pl.multiple_of(jnp.where(first, 0, half), half), half)
        weight_re = weight[:, 0:1]
        weight_im = weight[:, 1:2]
        recorded_re = piece_ref[0].astype(jnp.float32)
        recorded_im = piece_ref[1].astype(jnp.float32)
        scaled_ref[rows, :width] = (weight_re * recorded_re - weight_im * recorded_im).astype(jnp.bfloat16)
        scaled_ref[rows, width:] = (weight_re * recorded_im + weight_im * recorded_re).astype(jnp.bfloat16)


def scale(place, source_term, pieces):
    _, rows, cols = pieces[0].shape
    return kernel_call(
        scale_kernel,
        jax.ShapeDtypeStruct((2 * rows, 2 * cols), jnp.bfloat16),
        [SMEM] + [VMEM] * 3,
        VMEM,
        (place, source_term, *pieces),
        12 * rows * cols,
        16 * rows * cols,
    )


def pick_kernel(place_ref, at_home_ref, away_ref, out_ref):
    home = place_ref[18] == 1

    @pl.when(home)
    def _():
        out_ref[...] = at_home_ref[...]

    @pl.when(jnp.logical_not(home))
    def _():
        out_ref[...] = away_ref[...]


def pick(place, at_home, away):
    return kernel_call(
        pick_kernel,
        jax.ShapeDtypeStruct(away.shape, away.dtype),
        [SMEM, VMEM, VMEM],
        VMEM,
        (place, at_home, away),
        0,
        6 * away.size,
    )


def product_kernel(place_ref, *refs, fill, slots, base, begun, finish, count):
    left, refs = (refs[:8], refs[8:]) if fill else (None, refs)
    held_ref, refs = (None, refs) if fill else (refs[0], refs[1:])
    first_ref, refs = (refs[0], refs[1:]) if begun else (None, refs)
    right, refs = refs[:count], refs[count:]
    if fill:
        held_ref, refs = refs[0], refs[1:]
        for e in range(8):
            held_ref[place_ref[e]] = left[e][...]
    out_ref = refs[0]
    total = refs[1] if finish else out_ref
    home = place_ref[18] == 1
    rows, depth = held_ref.shape[2], held_ref.shape[3]

    def row_block(s):
        return held_ref[s if base is None else place_ref[base + s]].reshape(2 * rows, depth)

    def panel(i):
        if i == 0 and count > len(slots):
            return jnp.where(home, right[0][...], right[count - 1][...])
        return right[i][...]

    for i in range(0, len(slots), 2):
        part = jnp.dot(
            jnp.concatenate([row_block(slots[i]), row_block(slots[i + 1])], axis=1),
            jnp.concatenate([panel(i), panel(i + 1)], axis=0),
            preferred_element_type=jnp.float32,
        )
        if i > 0:
            total[...] += part
        elif begun:
            total[...] = first_ref[...] + part
        else:
            total[...] = part
    if finish:
        cols = out_ref.shape[2]
        out_ref[0] = (total[:rows, :cols] - total[rows:, cols:]).astype(out_ref.dtype)
        out_ref[1] = (total[:rows, cols:] + total[rows:, :cols]).astype(out_ref.dtype)


def product(place, left, right, slots, base=None, first=None, dtype=None):
    fill = isinstance(left, dict)
    lefts = [left[e] for e in range(8)] if fill else [left]
    rows, depth = lefts[0].shape[-2:]
    wide = right[0].shape[1]
    args = (place, *lefts, *([] if first is None else [first]), *right)
    out_shape = [jax.ShapeDtypeStruct((8, 2, rows, depth), jnp.bfloat16)] if fill else []
    scratch = []
    if dtype is None:
        out_shape.append(jax.ShapeDtypeStruct((2 * rows, wide), jnp.float32))
    else:
        out_shape.append(jax.ShapeDtypeStruct((2, rows, wide // 2), dtype))
        scratch = [pltpu.VMEM((2 * rows, wide), jnp.float32)]
    out = kernel_call(
        functools.partial(
            product_kernel,
            fill=fill,
            slots=slots,
            base=base,
            begun=first is not None,
            finish=dtype is not None,
            count=len(right),
        ),
        out_shape,
        [SMEM] + [VMEM] * (len(args) - 1),
        [VMEM] * len(out_shape),
        args,
        4 * len(slots) * rows * depth * wide,
        2 * len(slots) * (2 * rows + wide) * depth,
        scratch,
        12,
    )
    return out if fill else out[0]


def combine_kernel(place_ref, own_ref, other_ref, data_ref, *refs, last):
    if last:
        ahead_ref, next_ref, mult_ref, pack_ref, sums_ref = refs
    else:
        mult_ref, sums_ref, edge_ref = refs
    mult_re = (own_ref[0] + other_ref[0].astype(jnp.float32)).astype(jnp.bfloat16)
    mult_im = (own_ref[1] + other_ref[1].astype(jnp.float32)).astype(jnp.bfloat16)
    mult_ref[0] = mult_re
    mult_ref[1] = mult_im
    rows, cols = mult_re.shape
    lane = lax.broadcasted_iota(jnp.int32, (1, cols), 1) // LINE
    slot = lax.broadcasted_iota(jnp.int32, (1, 128), 1)
    for i in range(rows // LINE):
        span = slice(i * LINE, (i + 1) * LINE)
        m_re = mult_re[span].astype(jnp.float32)
        m_im = mult_im[span].astype(jnp.float32)
        d_re = data_ref[0, span].astype(jnp.float32)
        d_im = data_ref[1, span].astype(jnp.float32)
        terms = (m_re * d_re + m_im * d_im, m_re * d_im - m_im * d_re, m_re * m_re + m_im * m_im)
        along = jnp.concatenate(
            [jnp.sum(term, axis=0, keepdims=True) for term in terms] + [jnp.zeros((1, cols), jnp.float32)], axis=0
        )
        part = jnp.zeros((4, 128), jnp.float32)
        for j in range(cols // LINE):
            block = jnp.sum(jnp.where(lane == j, along, 0.0), axis=1, keepdims=True)
            part = jnp.where(slot == j, block, part)
        sums_ref[pl.ds(4 * i, 4), :] = part
    upper = place_ref[16] == 0
    count = sums_ref.shape[0]
    if last:
        pack_ref[:count] = jnp.where(upper, ahead_ref[...], sums_ref[...])
        pack_ref[count : 2 * count] = jnp.where(upper, sums_ref[...], ahead_ref[...])
        pack_ref[2 * count : 2 * count + 4] = next_ref[...]
        pack_ref[2 * count + 4 :] = jnp.zeros_like(next_ref)
    else:
        edge_ref[...] = jnp.where(upper, sums_ref[:4], sums_ref[count - 4 :])


def combine(place, own, other, data, ahead=None, from_next=None):
    _, rows, cols = own.shape
    count = 4 * (rows // LINE)
    args = (place, own, other, data)
    mult = jax.ShapeDtypeStruct((2, rows, cols), jnp.bfloat16)
    sums = jax.ShapeDtypeStruct((count, 128), jnp.float32)
    if ahead is None:
        out_shape = [mult, sums, jax.ShapeDtypeStruct((4, 128), jnp.float32)]
        scratch = []
    else:
        args += (ahead, from_next)
        out_shape = [mult, jax.ShapeDtypeStruct((2 * count + 8, 128), jnp.float32)]
        scratch = [pltpu.VMEM((count, 128), jnp.float32)]
    return kernel_call(
        functools.partial(combine_kernel, last=ahead is not None),
        out_shape,
        [SMEM] + [VMEM] * (len(args) - 1),
        [VMEM] * len(out_shape),
        args,
        16 * rows * cols,
        24 * rows * cols,
        scratch,
    )


def window_kernel(place_ref, mine_ref, mate_ref, out_ref):
    upper = place_ref[16] == 0
    mine, mate = mine_ref[...], mate_ref[...]
    first = jnp.where(upper, mine, mate)
    second = jnp.where(upper, mate, mine)
    count = first.shape[0] - 8
    tall = jnp.concatenate(
        [first[count : count + 4], first[:count], second[:count], second[count : count + 4]], axis=0
    )
    out_ref[...] = tall[: 2 * count] + tall[4 : 2 * count + 4] + tall[8:]


def apply_kernel(place_ref, *refs):
    mults = refs[:2]
    window_ref, heard_ref, mate_ref, out_ref, filtered, sems = refs[2:]
    copies = []
    lower = place_ref[17] == 0
    upper = place_ref[16] == 0
    count = window_ref.shape[0] // 2
    heard, mate = heard_ref[...], mate_ref[...]
    across = jnp.where(upper, heard[:count], mate[count:])
    other = jnp.where(upper, mate[:count], heard[count:])
    left = jnp.where(lower, other, across)
    right = jnp.where(lower, across, other)
    window = jnp.where(upper, window_ref[:count], window_ref[count:])
    slot = lax.broadcasted_iota(jnp.int32, window.shape, 1)
    cols = out_ref.shape[2]
    last = cols // LINE - 1
    before = jnp.where(slot == 0, pltpu.roll(left, 128 - last, 1), pltpu.roll(window, 1, 1))
    after = jnp.where(slot == last, pltpu.roll(right, last, 1), pltpu.roll(window, 127, 1))
    window = window + before + after
    lane = lax.broadcasted_iota(jnp.int32, (1, cols), 1) // LINE
    core = place_ref[16]
    half = window.shape[0] // 2
    rows = mults[0].shape[1]
    for r, mult_ref in enumerate(mults):
        chunk = jnp.where(core == r, window[:half], window[half:])
        start = jnp.where(core == r, 0, rows)
        for i in range(rows // LINE):
            energy = chunk[4 * i + 2 : 4 * i + 3] + STABILISER
            value = chunk[4 * i : 4 * i + 2] / energy
            spread = jnp.zeros((2, cols), jnp.float32)
            for j in range(last + 1):
                spread = jnp.where(lane == j, value[:, j : j + 1], spread)
            coef_re, coef_im = spread[0:1], spread[1:2]
            span = pl.ds(i * LINE, LINE)
            m_re = mult_ref[0, span].astype(jnp.float32)
            m_im = mult_ref[1, span].astype(jnp.float32)
            filtered[r, 0, span] = (coef_re * m_re - coef_im * m_im).astype(jnp.bfloat16)
            filtered[r, 1, span] = (coef_re * m_im + coef_im * m_re).astype(jnp.bfloat16)
            into = out_ref.at[:, pl.ds(pl.multiple_of(start + i * LINE, LINE), LINE)]
            copies.append(pltpu.make_async_copy(filtered.at[r, :, span], into, sems.at[r, i]))
            copies[-1].start()
    for copy in copies:
        copy.wait()


def on_device(data, source_term):
    piece0, piece1, place = begin(data)
    pieces = [piece0, piece1]
    scaled = scale(place, source_term, pieces)
    left = [{0: piece} for piece in pieces]
    up = list(pieces)
    down = list(pieces)
    for step in range(1, 5):
        for r in range(2):
            if step < 4 or r == 0:
                up[r] = send(up[r], z_up)
                left[r][step] = up[r]
            if step < 4 or r == 1:
                down[r] = send(down[r], z_down)
                left[r][8 - step] = down[r]

    near = send(scaled, near_y)
    far = send(scaled, far_y)

    hs = send(scaled, swap_core)
    h = pick(place, scaled, hs)
    h1 = send(h, x_apart)
    h2 = send(scaled, home_to_opposite)
    h1s = send(h1, swap_core)
    h2s = send(h2, swap_core)

    f = pick(place, near, far)
    fs = send(f, swap_core)
    f1a = send(f, x_apart)
    f1b = send(fs, x_apart)
    f2 = send(f1a, x_apart)
    f1as = send(f1a, swap_core)
    f1bs = send(f1b, swap_core)
    f2s = send(f2, swap_core)

    na = send(h1, y_beside)
    nb = send(pick(place, h2, h), y_beside)
    nas = send(na, swap_core)
    nbs = send(nb, swap_core)

    held0, part = product(place, left[0], [f, f1a, f1bs, fs, f1b, f1as], (0, 1, 3, 4, 5, 7))
    part = product(place, held0, [f2, f2s], (2, 6), None, part, PARTIAL)
    other0 = send(part, y_across)
    every = [f, f1a, f2, f1bs, fs, f1b, f2s, f1as]
    held1, part = product(place, left[1], every, tuple(range(8)), None, None, PARTIAL)
    other1 = send(part, y_across)
    every = [h2, nb, h, h1, h1s, nbs, na, nas, h2s]
    own0 = product(place, held0, every, tuple(range(8)), 8, None, jnp.float32)
    own1 = product(place, held1, every, tuple(range(8)), 8, None, jnp.float32)

    mult0, sums, edge = combine(place, own0, other0, pieces[0])
    from_next = send(edge, next_src)
    mult1, pack = combine(place, own1, other1, pieces[1], sums, from_next)
    from_mate = send(pack, swap_core)
    window = kernel_call(
        window_kernel,
        jax.ShapeDtypeStruct((2 * (pack.shape[0] - 8), 128), jnp.float32),
        [SMEM] + [VMEM] * 2,
        VMEM,
        (place, pack, from_mate),
    )
    heard = send(window, beside_rcv)
    from_mate = send(heard, swap_core)
    return kernel_call(
        apply_kernel,
        jax.ShapeDtypeStruct(data.shape, jnp.bfloat16),
        [SMEM] + [VMEM] * 5,
        pl.BlockSpec(memory_space=pl.ANY),
        (place, mult0, mult1, window, heard, from_mate),
        12 * data.shape[1] * data.shape[2],
        8 * data.shape[1] * data.shape[2],
        [pltpu.VMEM((2, *mult0.shape), jnp.bfloat16), pltpu.SemaphoreType.DMA((2, 3))],
    )


def solution(mesh):
    in_specs = (P(None, "src", "rcv"), P(None, "src"))
    out_specs = P(None, "src", "rcv")
    return jax.shard_map(
        on_device, mesh=mesh, in_specs=in_specs, out_specs=out_specs, check_vma=False
    )
```

```python
import functools

import jax
import jax.numpy as jnp
from jax import lax
from jax.experimental import pallas as pl
from jax.experimental.pallas import tpu as pltpu
from jax.sharding import PartitionSpec as P


LINE = 64
STABILISER = 1e-05
AXES = ("src", "rcv")
NX, NY, NZ = 4, 4, 8
PARTIAL = jnp.bfloat16
VMEM = pl.BlockSpec(memory_space=pltpu.VMEM)


def linear(x, y, z, core):
    return ((x * 2 + y % 2) * 2 + core) * 16 + z * 2 + y // 2


def send(value, target):
    pairs = []
    for x in range(NX):
        for y in range(NY):
            for z in range(NZ):
                for core in range(2):
                    to = target(x, y, z, core)
                    if to is not None:
                        pairs.append((linear(x, y, z, core), linear(to[0] % NX, to[1] % NY, to[2] % NZ, to[3])))
    return lax.ppermute(value, AXES, pairs)


def z_up(x, y, z, core):
    return x, y, z + 1, core


def z_down(x, y, z, core):
    return x, y, z - 1, core


def x_apart(x, y, z, core):
    return x + 1 - 2 * core, y, z, core


def home_to_opposite(x, y, z, core):
    return (x + 2, y, z, core) if core == y // 2 else None


def swap_core(x, y, z, core):
    return x, y, z, 1 - core


def y_across(x, y, z, core):
    return x, y + 2, z, core


def near_y(x, y, z, core):
    if y // 2 == core:
        return None
    return x, 3 - y, z, core


def y_beside(x, y, z, core):
    return x, y ^ 1, z, core


def far_y(x, y, z, core):
    if y // 2 == core:
        return None
    return x, y ^ 2, z, 1 - core


def next_src(x, y, z, core):
    src = (x * 2 + y % 2) * 2 + core + (1 if core else -1)
    if not 0 <= src < 16:
        return None
    return src // 4, y // 2 * 2 + src // 2 % 2, z, src % 2


def beside_rcv(x, y, z, core):
    if core == 0:
        return y_across(x, y, z, core)
    rcv = z * 2 + y // 2 + (1 if y // 2 else -1)
    if not 0 <= rcv < 16:
        return None
    return x, rcv % 2 * 2 + y % 2, rcv // 2, core


def kernel_call(kernel, out_shape, in_specs, out_specs, args, flops=0, moved=0, scratch=(), limit=8):
    return pl.pallas_call(
        lambda *refs: kernel(find_place(), *refs),
        out_shape=out_shape,
        in_specs=in_specs,
        out_specs=out_specs,
        scratch_shapes=scratch,
        compiler_params=pltpu.CompilerParams(vmem_limit_bytes=limit << 20),
        cost_estimate=pl.CostEstimate(flops=flops, bytes_accessed=moved, transcendentals=0),
    )(*args)


def find_place():
    src = lax.axis_index("src")
    rcv = lax.axis_index("rcv")
    x, y_lo, core = src >> 2, (src >> 1) & 1, src & 1
    z, y_hi = rcv >> 1, rcv & 1
    home = jnp.where(core == y_hi, 1, 0)
    place = []
    for e in range(8):
        block = (z - e) & 7
        shift_x = (x - (block >> 1)) & 3
        shift_x = jnp.where(core == 0, shift_x, (4 - shift_x) & 3)
        shift_y = (block & 1) ^ y_lo
        place.append(jnp.where(shift_y == home, 0, 4) + shift_x)
    at, away = 2 * home, 2 - 2 * home
    for shift_y, shift_x in ((0, 2), (1, at), (0, 0), (0, 1), (0, 3), (1, away), (1, 1), (1, 3)):
        place.append(jnp.where(home == shift_y, 0, 4) + shift_x)
    return [*place, core, y_hi, home]


def begin_kernel(place, data_ref, piece0_ref, piece1_ref):
    half = data_ref.shape[1] // 2
    for r, piece_ref in enumerate((piece0_ref, piece1_ref)):
        start = pl.multiple_of((place[16] if r == 0 else 1 - place[16]) * half, half)
        piece_ref[...] = data_ref[:, pl.ds(start, half)]


def begin(data):
    _, rows, cols = data.shape
    piece = jax.ShapeDtypeStruct((2, rows // 2, cols), jnp.bfloat16)
    return kernel_call(begin_kernel, (piece, piece), [VMEM], [VMEM, VMEM], (data,), 0, 8 * rows * cols)


def scale_kernel(place, source_ref, piece0_ref, piece1_ref, scaled_ref):
    weights = jnp.transpose(jnp.concatenate([source_ref[...]] * 4, axis=0))
    _, half, width = piece0_ref.shape
    for r, piece_ref in enumerate((piece0_ref, piece1_ref)):
        first = place[16] == r
        weight = jnp.where(first, weights[:half], weights[half:])
        rows = pl.ds(pl.multiple_of(jnp.where(first, 0, half), half), half)
        weight_re = weight[:, 0:1]
        weight_im = weight[:, 1:2]
        recorded_re = piece_ref[0].astype(jnp.float32)
        recorded_im = piece_ref[1].astype(jnp.float32)
        scaled_ref[rows, :width] = (weight_re * recorded_re - weight_im * recorded_im).astype(jnp.bfloat16)
        scaled_ref[rows, width:] = (weight_re * recorded_im + weight_im * recorded_re).astype(jnp.bfloat16)


def scale(source_term, pieces):
    _, rows, cols = pieces[0].shape
    return kernel_call(
        scale_kernel,
        jax.ShapeDtypeStruct((2 * rows, 2 * cols), jnp.bfloat16),
        [VMEM] * 3,
        VMEM,
        (source_term, *pieces),
        12 * rows * cols,
        16 * rows * cols,
    )


def pick_kernel(place, at_home_ref, away_ref, out_ref):
    home = place[18] == 1

    @pl.when(home)
    def _():
        out_ref[...] = at_home_ref[...]

    @pl.when(jnp.logical_not(home))
    def _():
        out_ref[...] = away_ref[...]


def pick(at_home, away):
    return kernel_call(
        pick_kernel,
        jax.ShapeDtypeStruct(away.shape, away.dtype),
        [VMEM, VMEM],
        VMEM,
        (at_home, away),
        0,
        6 * away.size,
    )


def product_kernel(place, *refs, fill, slots, base, begun, finish, count):
    left, refs = (refs[:8], refs[8:]) if fill else (None, refs)
    held_ref, refs = (None, refs) if fill else (refs[0], refs[1:])
    first_ref, refs = (refs[0], refs[1:]) if begun else (None, refs)
    right, refs = refs[:count], refs[count:]
    if fill:
        held_ref, refs = refs[0], refs[1:]
        for e in range(8):
            held_ref[place[e]] = left[e][...]
    out_ref = refs[0]
    total = refs[1] if finish else out_ref
    home = place[18] == 1
    rows, depth = held_ref.shape[2], held_ref.shape[3]

    def row_block(s):
        return held_ref[s if base is None else place[base + s]].reshape(2 * rows, depth)

    def panel(i):
        if i == 0 and count > len(slots):
            return jnp.where(home, right[0][...], right[count - 1][...])
        return right[i][...]

    for i in range(0, len(slots), 2):
        part = jnp.dot(
            jnp.concatenate([row_block(slots[i]), row_block(slots[i + 1])], axis=1),
            jnp.concatenate([panel(i), panel(i + 1)], axis=0),
            preferred_element_type=jnp.float32,
        )
        if i > 0:
            total[...] += part
        elif begun:
            total[...] = first_ref[...] + part
        else:
            total[...] = part
    if finish:
        cols = out_ref.shape[2]
        out_ref[0] = (total[:rows, :cols] - total[rows:, cols:]).astype(out_ref.dtype)
        out_ref[1] = (total[:rows, cols:] + total[rows:, :cols]).astype(out_ref.dtype)


def product(left, right, slots, base=None, first=None, dtype=None):
    fill = isinstance(left, dict)
    lefts = [left[e] for e in range(8)] if fill else [left]
    rows, depth = lefts[0].shape[-2:]
    wide = right[0].shape[1]
    args = (*lefts, *([] if first is None else [first]), *right)
    out_shape = [jax.ShapeDtypeStruct((8, 2, rows, depth), jnp.bfloat16)] if fill else []
    scratch = []
    if dtype is None:
        out_shape.append(jax.ShapeDtypeStruct((2 * rows, wide), jnp.float32))
    else:
        out_shape.append(jax.ShapeDtypeStruct((2, rows, wide // 2), dtype))
        scratch = [pltpu.VMEM((2 * rows, wide), jnp.float32)]
    out = kernel_call(
        functools.partial(
            product_kernel,
            fill=fill,
            slots=slots,
            base=base,
            begun=first is not None,
            finish=dtype is not None,
            count=len(right),
        ),
        out_shape,
        [VMEM] * len(args),
        [VMEM] * len(out_shape),
        args,
        4 * len(slots) * rows * depth * wide,
        2 * len(slots) * (2 * rows + wide) * depth,
        scratch,
        12,
    )
    return out if fill else out[0]


def combine_kernel(place, own_ref, other_ref, data_ref, *refs, last):
    if last:
        ahead_ref, next_ref, mult_ref, pack_ref, sums_ref = refs
    else:
        mult_ref, sums_ref, edge_ref = refs
    mult_re = (own_ref[0] + other_ref[0].astype(jnp.float32)).astype(jnp.bfloat16)
    mult_im = (own_ref[1] + other_ref[1].astype(jnp.float32)).astype(jnp.bfloat16)
    mult_ref[0] = mult_re
    mult_ref[1] = mult_im
    rows, cols = mult_re.shape
    lane = lax.broadcasted_iota(jnp.int32, (1, cols), 1) // LINE
    slot = lax.broadcasted_iota(jnp.int32, (1, 128), 1)
    for i in range(rows // LINE):
        span = slice(i * LINE, (i + 1) * LINE)
        m_re = mult_re[span].astype(jnp.float32)
        m_im = mult_im[span].astype(jnp.float32)
        d_re = data_ref[0, span].astype(jnp.float32)
        d_im = data_ref[1, span].astype(jnp.float32)
        terms = (m_re * d_re + m_im * d_im, m_re * d_im - m_im * d_re, m_re * m_re + m_im * m_im)
        along = jnp.concatenate(
            [jnp.sum(term, axis=0, keepdims=True) for term in terms] + [jnp.zeros((1, cols), jnp.float32)], axis=0
        )
        part = jnp.zeros((4, 128), jnp.float32)
        for j in range(cols // LINE):
            block = jnp.sum(jnp.where(lane == j, along, 0.0), axis=1, keepdims=True)
            part = jnp.where(slot == j, block, part)
        sums_ref[pl.ds(4 * i, 4), :] = part
    upper = place[16] == 0
    count = sums_ref.shape[0]
    if last:
        pack_ref[:count] = jnp.where(upper, ahead_ref[...], sums_ref[...])
        pack_ref[count : 2 * count] = jnp.where(upper, sums_ref[...], ahead_ref[...])
        pack_ref[2 * count : 2 * count + 4] = next_ref[...]
        pack_ref[2 * count + 4 :] = jnp.zeros_like(next_ref)
    else:
        edge_ref[...] = jnp.where(upper, sums_ref[:4], sums_ref[count - 4 :])


def combine(own, other, data, ahead=None, from_next=None):
    _, rows, cols = own.shape
    count = 4 * (rows // LINE)
    args = (own, other, data)
    mult = jax.ShapeDtypeStruct((2, rows, cols), jnp.bfloat16)
    sums = jax.ShapeDtypeStruct((count, 128), jnp.float32)
    if ahead is None:
        out_shape = [mult, sums, jax.ShapeDtypeStruct((4, 128), jnp.float32)]
        scratch = []
    else:
        args += (ahead, from_next)
        out_shape = [mult, jax.ShapeDtypeStruct((2 * count + 8, 128), jnp.float32)]
        scratch = [pltpu.VMEM((count, 128), jnp.float32)]
    return kernel_call(
        functools.partial(combine_kernel, last=ahead is not None),
        out_shape,
        [VMEM] * len(args),
        [VMEM] * len(out_shape),
        args,
        16 * rows * cols,
        24 * rows * cols,
        scratch,
    )


def window_kernel(place, mine_ref, mate_ref, out_ref):
    upper = place[16] == 0
    mine, mate = mine_ref[...], mate_ref[...]
    first = jnp.where(upper, mine, mate)
    second = jnp.where(upper, mate, mine)
    count = first.shape[0] - 8
    tall = jnp.concatenate(
        [first[count : count + 4], first[:count], second[:count], second[count : count + 4]], axis=0
    )
    out_ref[...] = tall[: 2 * count] + tall[4 : 2 * count + 4] + tall[8:]


def apply_kernel(place, *refs):
    mults = refs[:2]
    window_ref, heard_ref, mate_ref, out_ref, filtered, sems = refs[2:]
    copies = []
    lower = place[17] == 0
    upper = place[16] == 0
    count = window_ref.shape[0] // 2
    heard, mate = heard_ref[...], mate_ref[...]
    across = jnp.where(upper, heard[:count], mate[count:])
    other = jnp.where(upper, mate[:count], heard[count:])
    left = jnp.where(lower, other, across)
    right = jnp.where(lower, across, other)
    window = jnp.where(upper, window_ref[:count], window_ref[count:])
    slot = lax.broadcasted_iota(jnp.int32, window.shape, 1)
    cols = out_ref.shape[2]
    last = cols // LINE - 1
    before = jnp.where(slot == 0, pltpu.roll(left, 128 - last, 1), pltpu.roll(window, 1, 1))
    after = jnp.where(slot == last, pltpu.roll(right, last, 1), pltpu.roll(window, 127, 1))
    window = window + before + after
    lane = lax.broadcasted_iota(jnp.int32, (1, cols), 1) // LINE
    core = place[16]
    half = window.shape[0] // 2
    rows = mults[0].shape[1]
    for r, mult_ref in enumerate(mults):
        chunk = jnp.where(core == r, window[:half], window[half:])
        start = jnp.where(core == r, 0, rows)
        for i in range(rows // LINE):
            energy = chunk[4 * i + 2 : 4 * i + 3] + STABILISER
            value = chunk[4 * i : 4 * i + 2] / energy
            spread = jnp.zeros((2, cols), jnp.float32)
            for j in range(last + 1):
                spread = jnp.where(lane == j, value[:, j : j + 1], spread)
            coef_re, coef_im = spread[0:1], spread[1:2]
            span = pl.ds(i * LINE, LINE)
            m_re = mult_ref[0, span].astype(jnp.float32)
            m_im = mult_ref[1, span].astype(jnp.float32)
            filtered[r, 0, span] = (coef_re * m_re - coef_im * m_im).astype(jnp.bfloat16)
            filtered[r, 1, span] = (coef_re * m_im + coef_im * m_re).astype(jnp.bfloat16)
            into = out_ref.at[:, pl.ds(pl.multiple_of(start + i * LINE, LINE), LINE)]
            copies.append(pltpu.make_async_copy(filtered.at[r, :, span], into, sems.at[r, i]))
            copies[-1].start()
    for copy in copies:
        copy.wait()


def on_device(data, source_term):
    piece0, piece1 = begin(data)
    pieces = [piece0, piece1]
    scaled = scale(source_term, pieces)
    left = [{0: piece} for piece in pieces]
    up = list(pieces)
    down = list(pieces)
    for step in range(1, 5):
        for r in range(2):
            if step < 4 or r == 0:
                up[r] = send(up[r], z_up)
                left[r][step] = up[r]
            if step < 4 or r == 1:
                down[r] = send(down[r], z_down)
                left[r][8 - step] = down[r]

    near = send(scaled, near_y)
    far = send(scaled, far_y)

    hs = send(scaled, swap_core)
    h = pick(scaled, hs)
    h1 = send(h, x_apart)
    h2 = send(scaled, home_to_opposite)
    h1s = send(h1, swap_core)
    h2s = send(h2, swap_core)

    f = pick(near, far)
    fs = send(f, swap_core)
    f1a = send(f, x_apart)
    f1b = send(fs, x_apart)
    f2 = send(f1a, x_apart)
    f1as = send(f1a, swap_core)
    f1bs = send(f1b, swap_core)
    f2s = send(f2, swap_core)

    na = send(h1, y_beside)
    nb = send(pick(h2, h), y_beside)
    nas = send(na, swap_core)
    nbs = send(nb, swap_core)

    held0, part = product(left[0], [f, f1a, f1bs, fs, f1b, f1as], (0, 1, 3, 4, 5, 7))
    part = product(held0, [f2, f2s], (2, 6), None, part, PARTIAL)
    other0 = send(part, y_across)
    every = [f, f1a, f2, f1bs, fs, f1b, f2s, f1as]
    held1, part = product(left[1], every, tuple(range(8)), None, None, PARTIAL)
    other1 = send(part, y_across)
    every = [h2, nb, h, h1, h1s, nbs, na, nas, h2s]
    own0 = product(held0, [h2, h, h1, h1s, h2s], (0, 2, 3, 4), 8)
    own0 = product(held0, [nb, nbs, na, nas], (1, 5, 6, 7), 8, own0, jnp.float32)
    own1 = product(held1, every, tuple(range(8)), 8, None, jnp.float32)

    mult0, sums, edge = combine(own0, other0, pieces[0])
    from_next = send(edge, next_src)
    mult1, pack = combine(own1, other1, pieces[1], sums, from_next)
    from_mate = send(pack, swap_core)
    window = kernel_call(
        window_kernel,
        jax.ShapeDtypeStruct((2 * (pack.shape[0] - 8), 128), jnp.float32),
        [VMEM] * 2,
        VMEM,
        (pack, from_mate),
    )
    heard = send(window, beside_rcv)
    from_mate = send(heard, swap_core)
    return kernel_call(
        apply_kernel,
        jax.ShapeDtypeStruct(data.shape, jnp.bfloat16),
        [VMEM] * 5,
        pl.BlockSpec(memory_space=pl.ANY),
        (mult0, mult1, window, heard, from_mate),
        12 * data.shape[1] * data.shape[2],
        8 * data.shape[1] * data.shape[2],
        [pltpu.VMEM((2, *mult0.shape), jnp.bfloat16), pltpu.SemaphoreType.DMA((2, 3))],
    )


def solution(mesh):
    in_specs = (P(None, "src", "rcv"), P(None, "src"))
    out_specs = P(None, "src", "rcv")
    return jax.shard_map(
        on_device, mesh=mesh, in_specs=in_specs, out_specs=out_specs, check_vma=False
    )
```
